256 devices in a mesh: sec: 32 (over z, x), op: 8 (over y, core).
Axes of the slice: x: 4, y: 4, z: 8, core: 2. Of those that a mesh axis runs over, the one named last changes fastest.
Arguments:
- wavefunction: bfloat16 [64, 512, 512], P('sec'), may hold values from -24 to 24
- left_blocks: bfloat16 [32, 64, 512, 512], P('op', 'sec'), may hold values from -5 to 5
- right_blocks: bfloat16 [32, 512, 512], P('op'), may hold values from -1 to 1
- charge_shifts: int32 [32], P('op'), may hold values from -2 to 2, as said below
- sector_rows: int32 [64], replicated, may hold values from 64 to 512, as said below
Outputs:
- next_vector: bfloat16 [64, 512, 512], P('sec')
- lanczos_coefficients: float32 [2, 3], replicated
The draws below stay inside these ranges and needn't reach their ends.
Inputs may be any that keep to these rules, and one draw needn't show every extreme that they name: `charge_shifts`: some term has offset 2, some has offset -2, and some has offset 0. `sector_rows`: multiples of 64; some sector has 512 rows.
All inputs are finite; a program needn't handle non-finite values.
Results may differ from the reference program's by a relative error of at most 0.025.
Values may be sent and summed in bfloat16 or wider, within the bound.
A program may use at most 64 MiB of HBM per device.

```python
import jax
import jax.numpy as jnp
from jax import lax

BLK = 512
NR = 512
TERM_DEV = 4
PRODUCTS = 3
SECTORS = 64
TERMS = 32
DMAX = 2
N_OP = 8


def draw_charge_shifts(key, part):
    key_values, key_placed = jax.random.split(jax.random.fold_in(key, 11))
    values = jax.random.randint(key_values, (TERMS,), -DMAX, DMAX + 1)
    placed = jax.random.permutation(key_placed, TERMS)
    values = values.at[placed[0]].set(DMAX).at[placed[1]].set(-DMAX).at[placed[2]].set(0)
    return values.astype(jnp.int32)


def draw_sector_rows(key, part):
    key_units, key_full = jax.random.split(jax.random.fold_in(key, 23))
    units = jax.random.randint(key_units, (SECTORS,), 1, 9)
    picked = jax.random.randint(key_full, (), 0, SECTORS)
    units = units.at[picked].set(8)
    return (units * (BLK // 8)).astype(jnp.int32)


def sector_ramp(low, ratio):
    place = jnp.arange(SECTORS, dtype=jnp.float32) / jnp.float32(SECTORS - 1)
    return low * jnp.exp(place * jnp.log(jnp.float32(ratio)))


def falling_ramp(low, ratio):
    place = 1.0 - jnp.arange(SECTORS, dtype=jnp.float32) / jnp.float32(SECTORS - 1)
    return low * jnp.exp(place * jnp.log(jnp.float32(ratio)))


def draw_wavefunction(key, part):
    inner = jax.random.fold_in(key, 31)
    noise = jnp.clip(jax.random.normal(inner, (SECTORS, BLK, NR), jnp.float32), -4.0, 4.0)
    ramp = falling_ramp(0.5, 6.0)
    return (noise * ramp[:, None, None]).astype(jnp.bfloat16)


def draw_left_blocks(key, part):
    inner = jax.random.fold_in(key, 37)
    noise = jnp.clip(jax.random.normal(inner, (TERMS, SECTORS, BLK, BLK), jnp.float32), -4.0, 4.0)
    ramp = sector_ramp(0.5, 8.0)
    rows = jnp.arange(BLK, dtype=jnp.int32)
    eye = (rows[:, None] == rows[None, :]).astype(jnp.float32)
    return (noise / jnp.sqrt(jnp.float32(BLK)) + ramp[None, :, None, None] * eye[None, None, :, :]).astype(jnp.bfloat16)


def draw_right_blocks(key, part):
    inner = jax.random.fold_in(key, 41)
    noise = jnp.clip(jax.random.normal(inner, (TERMS, NR, NR), jnp.float32), -4.0, 4.0)
    strength = 2.0
    rows = jnp.arange(NR, dtype=jnp.int32)
    eye = (rows[:, None] == rows[None, :]).astype(jnp.float32)
    return (noise / jnp.sqrt(jnp.float32(NR * TERMS)) + strength / TERMS * eye[None, :, :]).astype(jnp.bfloat16)


def setup_inputs(seed: int = 0) -> dict:
    key_list = jax.random.split(jax.random.key(seed), 6)
    wavefunction = draw_wavefunction(jax.random.fold_in(key_list[5], 71), 0)
    left_blocks = draw_left_blocks(jax.random.fold_in(key_list[5], 71), 0)
    right_blocks = draw_right_blocks(jax.random.fold_in(key_list[5], 71), 0)
    charge_shifts = draw_charge_shifts(jax.random.fold_in(key_list[5], 71), 0)
    sector_rows = draw_sector_rows(jax.random.fold_in(key_list[5], 71), 0)
    return dict(wavefunction=wavefunction, left_blocks=left_blocks, right_blocks=right_blocks, charge_shifts=charge_shifts, sector_rows=sector_rows)


def apply_terms(vector, left_blocks, right_blocks, charge_shifts, row_mask):
    zeros_pad = jnp.zeros((DMAX, BLK, NR), jnp.bfloat16)
    padded = jnp.concatenate([zeros_pad, vector, zeros_pad], axis=0)
    total = jnp.zeros((SECTORS, BLK, NR), jnp.float32)
    for group in range(N_OP):

        def one_term(carry, term):
            shift = lax.dynamic_index_in_dim(charge_shifts, term, 0, keepdims=False)
            window = lax.dynamic_slice_in_dim(padded, (DMAX - shift).astype(jnp.int32), SECTORS, 0)
            right_mat = lax.dynamic_index_in_dim(right_blocks, term, 0, keepdims=False)
            left_mat = lax.dynamic_index_in_dim(left_blocks, term, 0, keepdims=False)
            right_part = jnp.einsum('sbn,nm->sbm', window.astype(jnp.float32), right_mat.astype(jnp.float32)).astype(jnp.bfloat16)
            return (carry + jnp.einsum('sab,sbm->sam', left_mat.astype(jnp.float32), right_part.astype(jnp.float32)), None)
        terms_list = jnp.arange(TERM_DEV, dtype=jnp.int32) + group * TERM_DEV
        partial_value, _ = lax.scan(one_term, jnp.zeros((SECTORS, BLK, NR), jnp.float32), terms_list)
        rounded = lax.optimization_barrier(partial_value.astype(jnp.bfloat16))
        total = total + rounded.astype(jnp.float32)
    return total * row_mask

def reference(wavefunction, left_blocks, right_blocks, charge_shifts, sector_rows):
    positions = jnp.arange(BLK, dtype=jnp.int32)
    row_mask = (positions[None, :] < sector_rows[:, None]).astype(jnp.float32)[:, :, None]
    live_count = NR * jnp.sum(sector_rows).astype(jnp.float32)
    masked_start = wavefunction.astype(jnp.float32) * row_mask
    vector = (masked_start / jnp.sqrt(jnp.sum(masked_start * masked_start) / live_count)).astype(jnp.bfloat16)
    previous = jnp.zeros((SECTORS, BLK, NR), jnp.float32)
    beta = jnp.float32(0.0)
    alphas = []
    betas = []
    for product in range(PRODUCTS):
        image = apply_terms(vector, left_blocks, right_blocks, charge_shifts, row_mask)
        current = vector.astype(jnp.float32)
        alpha = jnp.sum(current * image) / live_count
        residual = image - alpha * current - beta * previous
        beta = jnp.sqrt(jnp.sum(residual * residual) / live_count)
        previous = current
        vector = (residual / beta).astype(jnp.bfloat16)
        alphas.append(alpha)
        betas.append(beta)
    return (vector, jnp.stack([jnp.stack(alphas), jnp.stack(betas)]))
```

```python
import functools

import jax
import jax.numpy as jnp
from jax import lax
from jax.experimental import pallas as pl
from jax.experimental.pallas import tpu as pltpu
from jax.sharding import PartitionSpec as P

MESH = pl.DeviceIdType.MESH
PRODUCTS = 3
F32 = jnp.float32
BF16 = jnp.bfloat16
QUARTERS = 4
ZERO_SLOT = 6
X_CHIPS = 4


class Places:
    def __init__(self, sec_size, op_size):
        self.sec_size, self.op_size = sec_size, op_size
        self.sec = lax.axis_index("sec")
        self.op = lax.axis_index("op")
        self.y, self.core = self.op // 2, self.op % 2
        self.z, self.x = self.sec // X_CHIPS, self.sec % X_CHIPS
        self.y_size = op_size // 2
        self.z_size = sec_size // X_CHIPS

    def sibling(self):
        return (self.sec, self.y * 2 + (1 - self.core))

    def along_y(self, step):
        return (self.sec, ((self.y + step + self.y_size) % self.y_size) * 2 + self.core)

    def along_sec(self, step):
        return ((self.sec + step + self.sec_size) % self.sec_size, self.op)

    def op_peer(self, step):
        return (self.op + step) % self.op_size

    def x_peer(self, step):
        return (self.x + step) % X_CHIPS

    def z_peer(self, step):
        return (self.z + step) % self.z_size


def lanczos_kernel(
    sec_size, op_size, shift_ref, rows_ref, wave_hbm, left_hbm, right_hbm, out_ref, coef_ref, *scratch
):
    scratch = list(scratch)
    take = lambda count: [scratch.pop(0) for _ in range(count)]
    left, right, parts = take(3)
    vectors = [take(QUARTERS) for _ in range(PRODUCTS)] + [take(QUARTERS)]
    sib_out, sib_in, y_out, y_in = take(4)
    shard_v, shard_h, shard_own = take(3)
    op_tiles, x_tiles, z_tiles = (take(PRODUCTS + 1) for _ in range(3))
    own = [None] + take(PRODUCTS)
    load_sem, ext_sem, sib_sem, rs_sib_sem, rs_y_sem, send_sem, op_sem, x_sem, z_sem, tile_sem = take(10)
    block, width = parts.shape[0] // 8, parts.shape[1]
    quarter = block // QUARTERS
    half = quarter // 2
    at = Places(sec_size, op_size)
    core = at.core
    sent = [0] * (PRODUCTS + 1)

    def row_start(r):
        return pl.multiple_of(((at.y + r) % QUARTERS) * quarter, quarter)

    loads = []
    for r in range(QUARTERS):
        for n, sector in enumerate((core, 1 - core)):
            loads.append(
                pltpu.make_async_copy(
                    wave_hbm.at[sector, pl.ds(row_start(r), quarter), :],
                    vectors[0][r].at[n * 3],
                    load_sem.at[2 * r + n],
                )
            )
    loads.append(pltpu.make_async_copy(right_hbm, right, load_sem.at[8]))
    loads.append(pltpu.make_async_copy(left_hbm, left, load_sem.at[9]))
    for copy in loads:
        copy.start()

    for k in range(PRODUCTS):
        for r in range(QUARTERS):
            vectors[k][r][ZERO_SLOT] = jnp.zeros((quarter, width), BF16)
    for copy in loads[:8]:
        copy.wait()

    barrier = pltpu.get_barrier_semaphore()
    partners = [(at.sec, at.op_peer(s)) for s in range(1, op_size)]
    partners += [(at.z * X_CHIPS + at.x_peer(s), at.op) for s in range(1, X_CHIPS)]
    partners += [(at.z_peer(s) * X_CHIPS + at.x, at.op) for s in range(1, at.z_size)]
    partners += [at.along_sec(1), at.along_sec(-1)]
    for partner in partners:
        pl.semaphore_signal(barrier, inc=1, device_id=partner, device_id_type=MESH)

    live_rows = lax.fori_loop(0, rows_ref.shape[0], lambda i, total: total + rows_ref[i], jnp.int32(0))
    live = jnp.full((1, 1), live_rows * width, jnp.int32).astype(F32)
    my_rows = rows_ref[2 * at.sec + core]

    pl.semaphore_wait(barrier, len(partners))

    flying = []

    def remote(src, dst, to, recv, pool):
        return pltpu.make_async_remote_copy(
            src_ref=src, dst_ref=dst, send_sem=send_sem.at[pool, sent[pool]], recv_sem=recv, device_id=to,
            device_id_type=MESH,
        )

    def launch(copy, pool):
        copy.start()
        flying.append(copy)
        sent[pool] += 1

    def piece(k, r, j, h):
        return vectors[k][r].at[j, pl.ds(h * half, half), :]

    def slot(k, side, mine):
        return side + (0 if mine else 3 if k < PRODUCTS else 1)

    def send_piece(k, side, r, h, kind):
        src = piece(k, r, slot(k, side, True), h)
        if k > 0 and side == 0 and r == 0:
            src = own[k].at[pl.ds(h * half, half), :]
        if kind == "sib":
            to, r_to, side_to, sem = at.sibling(), r, side, sib_sem
        elif kind == "y+":
            to, r_to, side_to, sem = at.along_y(1), (r - 1) % QUARTERS, side, ext_sem
        elif kind == "y-":
            to, r_to, side_to, sem = at.along_y(-1), (r + 1) % QUARTERS, side, ext_sem
        elif kind == "x+":
            to, r_to, side_to, sem = at.along_sec(1), r, 1, ext_sem
        else:
            to, r_to, side_to, sem = at.along_sec(-1), r, 2, ext_sem
        dst = piece(k, r_to, slot(k, side_to, kind != "sib"), h)
        launch(remote(src, dst, to, sem.at[k, r_to, side_to, h], k), k)

    def wait_piece(k, side, r, h, sem, mine):
        here = piece(k, r, slot(k, side, mine), h)
        remote(here, here, at.sibling(), sem.at[k, r, side, h], k).wait_recv()

    def arrive(k, side, r, h, kinds):
        wait_piece(k, side, r, h, ext_sem, True)
        for kind in kinds:
            send_piece(k, side, r, h, kind)

    def right_products(k, r):
        first = row_start(r)
        ids = first + lax.broadcasted_iota(jnp.int32, (quarter, 1), 0)

        def body(term, carry):
            for target in range(2):
                shift = shift_ref[term]
                source = 2 * at.sec + target - shift
                valid = jnp.logical_and(source >= 0, source < 2 * sec_size)
                offset = target - shift
                side = jnp.where(offset < 0, 1, jnp.where(offset > 1, 2, 0))
                j = jnp.where((offset + 2) % 2 == core, side, side + 3)
                j = jnp.where(valid, j, ZERO_SLOT)
                value = jnp.dot(vectors[k][r][j], right[term], preferred_element_type=F32)
                if k == 0:
                    limit = rows_ref[jnp.clip(source, 0, 2 * sec_size - 1)]
                    value = jnp.where(ids < limit, value, 0.0)
                place = pl.multiple_of((term * 2 + target) * block + first, quarter)
                parts[pl.ds(place, quarter), :] = value.astype(BF16)
            return carry

        lax.fori_loop(0, 4, body, 0)

    def left_products(target, r):
        first = row_start(r)
        total = None
        for term in range(4):
            place = pl.multiple_of((term * 2 + target) * block, block)
            value = jnp.dot(
                left[term, target, pl.ds(first, quarter), :],
                parts[pl.ds(place, block), :],
                preferred_element_type=F32,
            )
            total = value if total is None else total + value
        return total

    def fold(value):
        folded = value[0:8]
        for i in range(8, value.shape[0], 8):
            folded = folded + value[i : i + 8]
        total = folded[:, 0:128]
        for i in range(128, width, 128):
            total = total + folded[:, i : i + 128]
        return total

    tile_count = [0] * (PRODUCTS + 1)

    def spread(tiles, sem, n, tile, count, partner):
        tiles[n][0] = tile
        for s in range(1, count):
            copy = pltpu.make_async_remote_copy(
                src_ref=tiles[n].at[0], dst_ref=tiles[n].at[count - s], send_sem=tile_sem.at[n, tile_count[n]],
                recv_sem=sem.at[n, count - s], device_id=partner(s), device_id_type=MESH,
            )
            copy.start()
            flying.append(copy)
            tile_count[n] += 1

    def gathered(tiles, sem, n, count, me):
        for s in range(1, count):
            pltpu.make_async_remote_copy(
                src_ref=tiles[n].at[s], dst_ref=tiles[n].at[s], send_sem=tile_sem.at[n, 0],
                recv_sem=sem.at[n, s], device_id=at.sibling(), device_id_type=MESH,
            ).wait_recv()
        total = None
        for i in range(count):
            tile = tiles[n][(i + count - me) % count]
            total = tile if total is None else total + tile
        return total

    def reduce_op(n, sums):
        tile = jnp.concatenate([jnp.sum(s, axis=0, keepdims=True) for s in sums], axis=0)
        tile = jnp.concatenate([tile, jnp.zeros((8 - len(sums), 128), F32)], axis=0)
        spread(op_tiles, op_sem, n, tile, op_size, lambda s: (at.sec, at.op_peer(s)))

    def reduce_x(n):
        tile = gathered(op_tiles, op_sem, n, op_size, at.op)
        spread(x_tiles, x_sem, n, tile, X_CHIPS, lambda s: (at.z * X_CHIPS + at.x_peer(s), at.op))

    def reduce_z(n):
        tile = gathered(x_tiles, x_sem, n, X_CHIPS, at.x)
        spread(z_tiles, z_sem, n, tile, at.z_size, lambda s: (at.z_peer(s) * X_CHIPS + at.x, at.op))

    def reduced(n):
        sums = jnp.sum(gathered(z_tiles, z_sem, n, at.z_size, at.z), axis=1, keepdims=True)
        return [sums[q : q + 1] / live for q in range(4)]

    step_rows = 32 if quarter % 32 == 0 else 16
    zero_sum = jnp.zeros((8, 128), F32)

    def blocks(body, carry):
        for first in range(0, quarter, step_rows):
            rows = pl.ds(first, step_rows)
            ids = at.y * quarter + first + lax.broadcasted_iota(jnp.int32, (step_rows, 1), 0)
            carry = body(rows, ids < my_rows, carry)
        return carry

    halo_y = {0: lambda r, h: r in (1, 3), 1: lambda r, h: r in (1, 3) and h == 1}
    via_y = lambda k, r, h: halo_y[min(k, 1)](r, h)

    for h in range(2):
        for kind in ("x+", "x-"):
            send_piece(0, 0, 0, h, kind)
    for h in range(2):
        for kind in ("x+", "x-"):
            send_piece(0, 0, 2, h, kind)

    def start_sum(rows, alive, carry):
        value = jnp.where(alive, vectors[0][0][0, rows, :].astype(F32), 0.0)
        return carry + fold(value * value)

    norm = blocks(start_sum, zero_sum)
    reduce_op(0, [norm, zero_sum, zero_sum, zero_sum])

    def halo_first(k):
        for h in range(2):
            for side in (1, 2):
                kinds = ["y+", "y-"] if via_y(k, 1, h) else []
                arrive(k, side, 0, h, kinds + ["sib"])

    def halo_rest(k, rs):
        for h in range(2):
            for r in rs:
                for side in (1, 2):
                    arrive(k, side, r, h, ["sib"])

    def from_sibling(k, sides, r):
        for side in sides:
            for h in range(2):
                wait_piece(k, side, r, h, sib_sem, False)

    alphas, betas = [], []
    shift_a = scale_b = guess = None
    combos = []
    for k in range(PRODUCTS):
        sides = (1, 2) if k == 0 else (0, 1, 2)
        if k > 0:
            for h in range(2):
                arrive(k, 0, 3, h, (["y+"] if h == 0 else []) + ([] if via_y(k, 3, h) else ["x+", "x-"]) + ["sib"])
                arrive(k, 0, 1, h, (["y-"] if h == 1 else []) + ([] if via_y(k, 1, h) else ["x+", "x-"]) + ["sib"])
        halo_first(k)
        if k > 0:
            for h in range(2):
                arrive(k, 0, 2, h, ["x+", "x-", "sib"])
        reduce_x(k)
        from_sibling(k, sides, 0)
        if k > 0:
            kept.wait()
        if k == 0:
            loads[8].wait()
        right_products(k, 0)
        halo_rest(k, (1, 3))
        reduce_z(k)
        from_sibling(k, sides, 1)
        right_products(k, 1)
        from_sibling(k, sides, 3)
        right_products(k, 3)
        halo_rest(k, (2,))
        from_sibling(k, sides, 2)
        right_products(k, 2)
        if k == 0:
            loads[9].wait()

        for r in (2, 1, 3, 0):
            sib_out[k, r] = left_products(1 - core, r).astype(BF16)
            launch(remote(sib_out.at[k, r], sib_in.at[k, r], at.sibling(), rs_sib_sem.at[k, r], k), k)
        for r in (2, 1, 3, 0):
            value = left_products(core, r)
            remote(sib_in.at[k, r], sib_in.at[k, r], at.sibling(), rs_sib_sem.at[k, r], k).wait_recv()
            value = value + sib_in[k, r].astype(F32)
            if r == 0:
                shard_own[...] = value
            else:
                y_out[k, r - 1] = value.astype(BF16)
                launch(
                    remote(y_out.at[k, r - 1], y_in.at[k, 3 - r], at.along_y(r), rs_y_sem.at[k, 3 - r], k), k
                )

        s = reduced(k)
        if k == 0:
            a, b = jnp.zeros((1, 1), F32), jnp.sqrt(s[0])
            guess = jnp.zeros((1, 1), F32)
            next_guess = guess
        else:
            alpha = s[0]
            a = alpha - guess
            b = jnp.sqrt(s[1] - 2.0 * a * s[2] + a * a * s[3])
            alphas.append(alpha)
            betas.append(b)
            next_guess = alpha
        inv_b = 1.0 / b
        combos.append((a, inv_b))
        beta = betas[-1] if k > 0 else jnp.zeros((1, 1), F32)
        guess = next_guess

        for i in range(3):
            remote(y_in.at[k, i], y_in.at[k, i], at.sibling(), rs_y_sem.at[k, i], k).wait_recv()


        def shard_step(rows, alive, carry):
            product = shard_own[rows, :]
            for i in range(3):
                product = product + y_in[k, i, rows, :].astype(F32)
            product = jnp.where(alive, product, 0.0)
            u = (vectors[0][0][0, rows, :] if k == 0 else own[k][rows, :]).astype(F32)
            if k == 0:
                v = jnp.where(alive, u, 0.0) * inv_b
                image = product * inv_b
                new = image
            else:
                v_before = shard_v[(k - 1) % 2, rows, :]
                v = (u - a * v_before) * inv_b
                image = (product - a * shard_h[rows, :]) * inv_b
                new = image - guess * v - beta * v_before
            shard_v[k % 2, rows, :] = v
            shard_h[rows, :] = image
            new = new.astype(BF16)
            own[k + 1][rows, :] = new
            new = new.astype(F32)
            pairs = ((v, image), (new, new), (new, v), (v, v))
            return tuple(c + fold(p * q) for c, (p, q) in zip(carry, pairs))

        sums = blocks(shard_step, (zero_sum,) * 4)
        kinds = ("y+", "y-", "x+", "x-", "sib") if k + 1 < PRODUCTS else ("y+", "y-", "sib")
        for h in range(2):
            for kind in kinds:
                send_piece(k + 1, 0, 0, h, kind)
        kept = pltpu.make_async_copy(own[k + 1], vectors[k + 1][0].at[0], load_sem.at[10 + k])
        kept.start()
        reduce_op(k + 1, sums)

    n = PRODUCTS
    for h in range(2):
        arrive(n, 0, 3, h, (["y+"] if h == 0 else []) + ["sib"])
        arrive(n, 0, 1, h, (["y-"] if h == 1 else []) + ["sib"])
    reduce_x(n)
    for h in range(2):
        arrive(n, 0, 2, h, ["sib"])
    reduce_z(n)
    for r in range(QUARTERS):
        from_sibling(n, (0,), r)
    kept.wait()
    s = reduced(n)
    a = s[0] - guess
    b = jnp.sqrt(s[1] - 2.0 * a * s[2] + a * a * s[3])
    alphas.append(s[0])
    betas.append(b)
    combos.append((a, 1.0 / b))

    weights = [None] * 4
    factor = combos[3][1]
    weights[3] = factor
    for i in (2, 1, 0):
        factor = -factor * combos[i + 1][0] * combos[i][1]
        weights[i] = factor
    for r in range(QUARTERS):
        first = row_start(r)
        for n, t in enumerate((core, 1 - core)):
            limit = rows_ref[2 * at.sec + t]

            def final(i, carry, r=r, n=n, t=t, limit=limit, first=first):
                rows = pl.ds(pl.multiple_of(i * step_rows, step_rows), step_rows)
                ids = first + i * step_rows + lax.broadcasted_iota(jnp.int32, (step_rows, 1), 0)
                value = jnp.where(ids < limit, vectors[0][r][3 * n, rows, :].astype(F32), 0.0) * weights[0]
                for m in (1, 2):
                    value = value + vectors[m][r][3 * n, rows, :].astype(F32) * weights[m]
                value = value + vectors[3][r][n, rows, :].astype(F32) * weights[3]
                out_ref[t, pl.ds(pl.multiple_of(first + i * step_rows, step_rows), step_rows), :] = value.astype(BF16)
                return carry

            lax.fori_loop(0, quarter // step_rows, final, 0)

    row = lax.broadcasted_iota(jnp.int32, (8, 128), 0)
    lane = lax.broadcasted_iota(jnp.int32, (8, 128), 1)
    coefs = jnp.zeros((8, 128), F32)
    for i in range(PRODUCTS):
        coefs = jnp.where((row == 0) & (lane == i), alphas[i], coefs)
        coefs = jnp.where((row == 1) & (lane == i), betas[i], coefs)
    coef_ref[...] = coefs

    for copy in flying:
        copy.wait_send()


def on_device(sec_size, op_size, wavefunction, left_blocks, right_blocks, charge_shifts, sector_rows):
    sectors_here, block, width = wavefunction.shape
    terms = left_blocks.shape[0]
    quarter = block // QUARTERS
    z_size = sec_size // X_CHIPS
    dma = pltpu.SemaphoreType.DMA
    scratch = [
        pltpu.VMEM(left_blocks.shape, BF16),
        pltpu.VMEM(right_blocks.shape, BF16),
        pltpu.VMEM((terms * sectors_here * block, width), BF16),
    ]
    scratch += [pltpu.VMEM((ZERO_SLOT + 1, quarter, width), BF16) for _ in range(PRODUCTS * QUARTERS)]
    scratch += [pltpu.VMEM((sectors_here, quarter, width), BF16) for _ in range(QUARTERS)]
    scratch += [pltpu.VMEM((PRODUCTS, QUARTERS, quarter, width), BF16)] * 2
    scratch += [pltpu.VMEM((PRODUCTS, 3, quarter, width), BF16)] * 2
    scratch += [
        pltpu.VMEM((2, quarter, width), F32),
        pltpu.VMEM((quarter, width), F32),
        pltpu.VMEM((quarter, width), F32),
    ]
    rounds = PRODUCTS + 1
    scratch += [pltpu.VMEM((count, 8, 128), F32) for count in (op_size, X_CHIPS, z_size) for _ in range(rounds)]
    scratch += [pltpu.VMEM((quarter, width), BF16) for _ in range(PRODUCTS)]
    scratch += [
        dma((10 + PRODUCTS,)),
        dma((rounds, QUARTERS, 3, 2)),
        dma((rounds, QUARTERS, 3, 2)),
        dma((PRODUCTS, QUARTERS)),
        dma((PRODUCTS, 3)),
        dma((rounds, 64)),
        dma((rounds, op_size)),
        dma((rounds, X_CHIPS)),
        dma((rounds, z_size)),
        dma((rounds, op_size + X_CHIPS + z_size)),
    ]
    smem = pl.BlockSpec(memory_space=pltpu.SMEM)
    hbm = pl.BlockSpec(memory_space=pl.ANY)
    vmem = pl.BlockSpec(memory_space=pltpu.VMEM)
    vector, coefs = pl.pallas_call(
        functools.partial(lanczos_kernel, sec_size, op_size),
        out_shape=(
            jax.ShapeDtypeStruct(wavefunction.shape, BF16),
            jax.ShapeDtypeStruct((8, 128), F32),
        ),
        in_specs=[smem, smem, hbm, hbm, hbm],
        out_specs=(vmem, vmem),
        scratch_shapes=scratch,
        compiler_params=pltpu.CompilerParams(
            collective_id=0, has_side_effects=True, vmem_limit_bytes=56 * 1024 * 1024
        ),
    )(charge_shifts, sector_rows, wavefunction, left_blocks, right_blocks)
    return vector, coefs[0:2, 0:PRODUCTS]


def solution(mesh):
    in_specs = (P("sec", None, None), P("op", "sec", None, None), P("op", None, None), P("op"), P())
    out_specs = (P("sec", None, None), P())
    return jax.shard_map(
        functools.partial(on_device, mesh.shape["sec"], mesh.shape["op"]),
        mesh=mesh, in_specs=in_specs, out_specs=out_specs, check_vma=False,
    )
```

```python
import functools

import jax
import jax.numpy as jnp
from jax import lax
from jax.experimental import pallas as pl
from jax.experimental.pallas import tpu as pltpu
from jax.sharding import PartitionSpec as P

MESH = pl.DeviceIdType.MESH
PRODUCTS = 3
F32 = jnp.float32
BF16 = jnp.bfloat16
QUARTERS = 4
ZERO_SLOT = 6
X_CHIPS = 4


class Places:
    def __init__(self, sec_size, op_size):
        self.sec_size, self.op_size = sec_size, op_size
        self.sec = lax.axis_index("sec")
        self.op = lax.axis_index("op")
        self.y, self.core = self.op // 2, self.op % 2
        self.z, self.x = self.sec // X_CHIPS, self.sec % X_CHIPS
        self.y_size = op_size // 2
        self.z_size = sec_size // X_CHIPS

    def sibling(self):
        return (self.sec, self.y * 2 + (1 - self.core))

    def along_y(self, step):
        return (self.sec, ((self.y + step + self.y_size) % self.y_size) * 2 + self.core)

    def along_sec(self, step):
        return ((self.sec + step + self.sec_size) % self.sec_size, self.op)

    def op_peer(self, step):
        return (self.op + step) % self.op_size

    def x_peer(self, step):
        return (self.x + step) % X_CHIPS

    def z_peer(self, step):
        return (self.z + step) % self.z_size


def lanczos_kernel(
    sec_size, op_size, shift_ref, rows_ref, wave_hbm, left_hbm, right_hbm, out_ref, coef_ref, *scratch
):
    scratch = list(scratch)
    take = lambda count: [scratch.pop(0) for _ in range(count)]
    left, right, parts = take(3)
    vectors = [take(QUARTERS) for _ in range(PRODUCTS)] + [take(QUARTERS)]
    sib_out, sib_in, y_out, y_in = take(4)
    shard_v, shard_h, shard_own = take(3)
    op_tiles, x_tiles, z_tiles = (take(PRODUCTS + 1) for _ in range(3))
    own = [None] + take(PRODUCTS)
    load_sem, ext_sem, sib_sem, rs_sib_sem, rs_y_sem, send_sem, op_sem, x_sem, z_sem, tile_sem = take(10)
    block, width = parts.shape[0] // 8, parts.shape[1]
    quarter = block // QUARTERS
    half = quarter // 2
    at = Places(sec_size, op_size)
    core = at.core
    sent = [0] * (PRODUCTS + 1)

    def row_start(r):
        return pl.multiple_of(((at.y + r) % QUARTERS) * quarter, quarter)

    loads = []
    for r in range(QUARTERS):
        for n, sector in enumerate((core, 1 - core)):
            loads.append(
                pltpu.make_async_copy(
                    wave_hbm.at[sector, pl.ds(row_start(r), quarter), :],
                    vectors[0][r].at[n * 3],
                    load_sem.at[2 * r + n],
                )
            )
    loads.append(pltpu.make_async_copy(right_hbm, right, load_sem.at[8]))
    loads.append(pltpu.make_async_copy(left_hbm, left, load_sem.at[9]))
    for copy in loads:
        copy.start()

    for k in range(PRODUCTS):
        for r in range(QUARTERS):
            vectors[k][r][ZERO_SLOT] = jnp.zeros((quarter, width), BF16)
    for copy in loads[:8]:
        copy.wait()

    barrier = pltpu.get_barrier_semaphore()
    partners = [(at.sec, at.op_peer(s)) for s in range(1, op_size)]
    partners += [(at.z * X_CHIPS + at.x_peer(s), at.op) for s in range(1, X_CHIPS)]
    partners += [(at.z_peer(s) * X_CHIPS + at.x, at.op) for s in range(1, at.z_size)]
    partners += [at.along_sec(1), at.along_sec(-1)]
    for partner in partners:
        pl.semaphore_signal(barrier, inc=1, device_id=partner, device_id_type=MESH)

    live_rows = lax.fori_loop(0, rows_ref.shape[0], lambda i, total: total + rows_ref[i], jnp.int32(0))
    live = jnp.full((1, 1), live_rows * width, jnp.int32).astype(F32)
    my_rows = rows_ref[2 * at.sec + core]

    pl.semaphore_wait(barrier, len(partners))

    flying = []

    def remote(src, dst, to, recv, pool):
        return pltpu.make_async_remote_copy(
            src_ref=src, dst_ref=dst, send_sem=send_sem.at[pool, sent[pool]], recv_sem=recv, device_id=to,
            device_id_type=MESH,
        )

    def launch(copy, pool):
        copy.start()
        flying.append(copy)
        sent[pool] += 1

    def piece(k, r, j, h):
        return vectors[k][r].at[j, pl.ds(h * half, half), :]

    def slot(k, side, mine):
        return side + (0 if mine else 3 if k < PRODUCTS else 1)

    def send_piece(k, side, r, h, kind):
        src = piece(k, r, slot(k, side, True), h)
        if k > 0 and side == 0 and r == 0:
            src = own[k].at[pl.ds(h * half, half), :]
        if kind == "sib":
            to, r_to, side_to, sem = at.sibling(), r, side, sib_sem
        elif kind == "y+":
            to, r_to, side_to, sem = at.along_y(1), (r - 1) % QUARTERS, side, ext_sem
        elif kind == "y-":
            to, r_to, side_to, sem = at.along_y(-1), (r + 1) % QUARTERS, side, ext_sem
        elif kind == "x+":
            to, r_to, side_to, sem = at.along_sec(1), r, 1, ext_sem
        else:
            to, r_to, side_to, sem = at.along_sec(-1), r, 2, ext_sem
        dst = piece(k, r_to, slot(k, side_to, kind != "sib"), h)
        launch(remote(src, dst, to, sem.at[k, r_to, side_to, h], k), k)

    def wait_piece(k, side, r, h, sem, mine):
        here = piece(k, r, slot(k, side, mine), h)
        remote(here, here, at.sibling(), sem.at[k, r, side, h], k).wait_recv()

    def arrive(k, side, r, h, kinds):
        wait_piece(k, side, r, h, ext_sem, True)
        for kind in kinds:
            send_piece(k, side, r, h, kind)

    def right_products(k, r):
        first = row_start(r)
        ids = first + lax.broadcasted_iota(jnp.int32, (quarter, 1), 0)

        def body(term):
            for target in range(2):
                shift = shift_ref[term]
                source = 2 * at.sec + target - shift
                valid = jnp.logical_and(source >= 0, source < 2 * sec_size)
                offset = target - shift
                side = jnp.where(offset < 0, 1, jnp.where(offset > 1, 2, 0))
                j = jnp.where((offset + 2) % 2 == core, side, side + 3)
                j = jnp.where(valid, j, ZERO_SLOT)
                value = jnp.dot(vectors[k][r][j], right[term], preferred_element_type=F32)
                if k == 0:
                    limit = rows_ref[jnp.clip(source, 0, 2 * sec_size - 1)]
                    value = jnp.where(ids < limit, value, 0.0)
                place = pl.multiple_of((term * 2 + target) * block + first, quarter)
                parts[pl.ds(place, quarter), :] = value.astype(BF16)

        for term in range(4):
            body(term)

    def left_products(target, r):
        first = row_start(r)
        total = None
        for term in range(4):
            place = pl.multiple_of((term * 2 + target) * block, block)
            value = jnp.dot(
                left[term, target, pl.ds(first, quarter), :],
                parts[pl.ds(place, block), :],
                preferred_element_type=F32,
            )
            total = value if total is None else total + value
        return total

    def fold(value):
        folded = value[0:8]
        for i in range(8, value.shape[0], 8):
            folded = folded + value[i : i + 8]
        total = folded[:, 0:128]
        for i in range(128, width, 128):
            total = total + folded[:, i : i + 128]
        return total

    tile_count = [0] * (PRODUCTS + 1)

    def spread(tiles, sem, n, tile, count, partner):
        tiles[n][0] = tile
        for s in range(1, count):
            copy = pltpu.make_async_remote_copy(
                src_ref=tiles[n].at[0], dst_ref=tiles[n].at[count - s], send_sem=tile_sem.at[n, tile_count[n]],
                recv_sem=sem.at[n, count - s], device_id=partner(s), device_id_type=MESH,
            )
            copy.start()
            flying.append(copy)
            tile_count[n] += 1

    def gathered(tiles, sem, n, count, me):
        for s in range(1, count):
            pltpu.make_async_remote_copy(
                src_ref=tiles[n].at[s], dst_ref=tiles[n].at[s], send_sem=tile_sem.at[n, 0],
                recv_sem=sem.at[n, s], device_id=at.sibling(), device_id_type=MESH,
            ).wait_recv()
        total = None
        for i in range(count):
            tile = tiles[n][(i + count - me) % count]
            total = tile if total is None else total + tile
        return total

    def reduce_op(n, sums):
        tile = jnp.concatenate([jnp.sum(s, axis=0, keepdims=True) for s in sums], axis=0)
        tile = jnp.concatenate([tile, jnp.zeros((8 - len(sums), 128), F32)], axis=0)
        spread(op_tiles, op_sem, n, tile, op_size, lambda s: (at.sec, at.op_peer(s)))

    def reduce_x(n):
        tile = gathered(op_tiles, op_sem, n, op_size, at.op)
        spread(x_tiles, x_sem, n, tile, X_CHIPS, lambda s: (at.z * X_CHIPS + at.x_peer(s), at.op))

    def reduce_z(n):
        tile = gathered(x_tiles, x_sem, n, X_CHIPS, at.x)
        spread(z_tiles, z_sem, n, tile, at.z_size, lambda s: (at.z_peer(s) * X_CHIPS + at.x, at.op))

    def reduced(n):
        sums = jnp.sum(gathered(z_tiles, z_sem, n, at.z_size, at.z), axis=1, keepdims=True)
        return [sums[q : q + 1] / live for q in range(4)]

    step_rows = 32 if quarter % 32 == 0 else 16
    zero_sum = jnp.zeros((8, 128), F32)

    def blocks(body, carry):
        for first in range(0, quarter, step_rows):
            rows = pl.ds(first, step_rows)
            ids = at.y * quarter + first + lax.broadcasted_iota(jnp.int32, (step_rows, 1), 0)
            carry = body(rows, ids < my_rows, carry)
        return carry

    halo_y = {0: lambda r, h: r in (1, 3), 1: lambda r, h: r in (1, 3) and h == 1}
    via_y = lambda k, r, h: halo_y[min(k, 1)](r, h)

    for h in range(2):
        for kind in ("x+", "x-"):
            send_piece(0, 0, 0, h, kind)
    for h in range(2):
        for kind in ("x+", "x-"):
            send_piece(0, 0, 2, h, kind)

    def start_sum(rows, alive, carry):
        value = jnp.where(alive, vectors[0][0][0, rows, :].astype(F32), 0.0)
        return carry + fold(value * value)

    norm = blocks(start_sum, zero_sum)
    reduce_op(0, [norm, zero_sum, zero_sum, zero_sum])

    def halo_first(k):
        for h in range(2):
            for side in (1, 2):
                kinds = ["y+", "y-"] if via_y(k, 1, h) else []
                arrive(k, side, 0, h, kinds + ["sib"])

    def halo_rest(k, rs):
        for h in range(2):
            for r in rs:
                for side in (1, 2):
                    arrive(k, side, r, h, ["sib"])

    def from_sibling(k, sides, r):
        for side in sides:
            for h in range(2):
                wait_piece(k, side, r, h, sib_sem, False)

    alphas, betas = [], []
    shift_a = scale_b = guess = None
    combos = []
    for k in range(PRODUCTS):
        sides = (1, 2) if k == 0 else (0, 1, 2)
        if k > 0:
            for h in range(2):
                arrive(k, 0, 3, h, (["y+"] if h == 0 else []) + ([] if via_y(k, 3, h) else ["x+", "x-"]) + ["sib"])
                arrive(k, 0, 1, h, (["y-"] if h == 1 else []) + ([] if via_y(k, 1, h) else ["x+", "x-"]) + ["sib"])
        halo_first(k)
        if k > 0:
            for h in range(2):
                arrive(k, 0, 2, h, ["x+", "x-", "sib"])
        reduce_x(k)
        from_sibling(k, sides, 0)
        if k > 0:
            kept.wait()
        if k == 0:
            loads[8].wait()
        right_products(k, 0)
        halo_rest(k, (1, 3))
        reduce_z(k)
        from_sibling(k, sides, 1)
        right_products(k, 1)
        from_sibling(k, sides, 3)
        halo_rest(k, (2,))
        right_products(k, 3)
        from_sibling(k, sides, 2)
        right_products(k, 2)
        if k == 0:
            loads[9].wait()

        def for_sibling(r):
            sib_out[k, r] = left_products(1 - core, r).astype(BF16)
            launch(remote(sib_out.at[k, r], sib_in.at[k, r], at.sibling(), rs_sib_sem.at[k, r], k), k)

        def for_chip(r):
            value = left_products(core, r)
            remote(sib_in.at[k, r], sib_in.at[k, r], at.sibling(), rs_sib_sem.at[k, r], k).wait_recv()
            value = value + sib_in[k, r].astype(F32)
            if r == 0:
                shard_own[...] = value
            else:
                y_out[k, r - 1] = value.astype(BF16)
                launch(
                    remote(y_out.at[k, r - 1], y_in.at[k, 3 - r], at.along_y(r), rs_y_sem.at[k, 3 - r], k), k
                )

        for_sibling(2)
        for_sibling(1)
        for_chip(2)
        for_sibling(3)
        for_chip(1)
        for_sibling(0)
        for_chip(3)
        for_chip(0)

        s = reduced(k)
        if k == 0:
            a, b = jnp.zeros((1, 1), F32), jnp.sqrt(s[0])
            guess = jnp.zeros((1, 1), F32)
            next_guess = guess
        else:
            alpha = s[0]
            a = alpha - guess
            b = jnp.sqrt(s[1] - 2.0 * a * s[2] + a * a * s[3])
            alphas.append(alpha)
            betas.append(b)
            next_guess = alpha
        inv_b = 1.0 / b
        combos.append((a, inv_b))
        beta = betas[-1] if k > 0 else jnp.zeros((1, 1), F32)
        guess = next_guess

        for i in range(3):
            remote(y_in.at[k, i], y_in.at[k, i], at.sibling(), rs_y_sem.at[k, i], k).wait_recv()


        def shard_step(rows, alive, carry):
            product = shard_own[rows, :]
            for i in range(3):
                product = product + y_in[k, i, rows, :].astype(F32)
            product = jnp.where(alive, product, 0.0)
            u = (vectors[0][0][0, rows, :] if k == 0 else own[k][rows, :]).astype(F32)
            if k == 0:
                v = jnp.where(alive, u, 0.0) * inv_b
                image = product * inv_b
                new = image
            else:
                v_before = shard_v[(k - 1) % 2, rows, :]
                v = (u - a * v_before) * inv_b
                image = (product - a * shard_h[rows, :]) * inv_b
                new = image - guess * v - beta * v_before
            shard_v[k % 2, rows, :] = v
            shard_h[rows, :] = image
            new = new.astype(BF16)
            own[k + 1][rows, :] = new
            new = new.astype(F32)
            pairs = ((v, image), (new, new), (new, v), (v, v))
            return tuple(c + fold(p * q) for c, (p, q) in zip(carry, pairs))

        sums = blocks(shard_step, (zero_sum,) * 4)
        kinds = ("y+", "y-", "x+", "x-", "sib") if k + 1 < PRODUCTS else ("y+", "y-", "sib")
        for h in range(2):
            for kind in kinds:
                send_piece(k + 1, 0, 0, h, kind)
        kept = pltpu.make_async_copy(own[k + 1], vectors[k + 1][0].at[0], load_sem.at[10 + k])
        kept.start()
        reduce_op(k + 1, sums)

    n = PRODUCTS
    arrive(n, 0, 3, 0, ["y+", "sib"])
    arrive(n, 0, 1, 0, ["sib"])
    reduce_x(n)
    arrive(n, 0, 3, 1, ["sib"])
    arrive(n, 0, 1, 1, ["y-", "sib"])
    reduce_z(n)
    for h in range(2):
        arrive(n, 0, 2, h, ["sib"])
    for r in range(QUARTERS):
        from_sibling(n, (0,), r)
    kept.wait()
    s = reduced(n)
    a = s[0] - guess
    b = jnp.sqrt(s[1] - 2.0 * a * s[2] + a * a * s[3])
    alphas.append(s[0])
    betas.append(b)
    combos.append((a, 1.0 / b))

    weights = [None] * 4
    factor = combos[3][1]
    weights[3] = factor
    for i in (2, 1, 0):
        factor = -factor * combos[i + 1][0] * combos[i][1]
        weights[i] = factor
    for r in range(QUARTERS):
        first = row_start(r)
        for n, t in enumerate((core, 1 - core)):
            limit = rows_ref[2 * at.sec + t]

            def final(i, carry, r=r, n=n, t=t, limit=limit, first=first):
                rows = pl.ds(pl.multiple_of(i * step_rows, step_rows), step_rows)
                ids = first + i * step_rows + lax.broadcasted_iota(jnp.int32, (step_rows, 1), 0)
                value = jnp.where(ids < limit, vectors[0][r][3 * n, rows, :].astype(F32), 0.0) * weights[0]
                for m in (1, 2):
                    value = value + vectors[m][r][3 * n, rows, :].astype(F32) * weights[m]
                value = value + vectors[3][r][n, rows, :].astype(F32) * weights[3]
                out_ref[t, pl.ds(pl.multiple_of(first + i * step_rows, step_rows), step_rows), :] = value.astype(BF16)
                return carry

            lax.fori_loop(0, quarter // step_rows, final, 0)

    row = lax.broadcasted_iota(jnp.int32, (8, 128), 0)
    lane = lax.broadcasted_iota(jnp.int32, (8, 128), 1)
    coefs = jnp.zeros((8, 128), F32)
    for i in range(PRODUCTS):
        coefs = jnp.where((row == 0) & (lane == i), alphas[i], coefs)
        coefs = jnp.where((row == 1) & (lane == i), betas[i], coefs)
    coef_ref[...] = coefs[0:2, 0:PRODUCTS]

    for copy in flying:
        copy.wait_send()


def on_device(sec_size, op_size, wavefunction, left_blocks, right_blocks, charge_shifts, sector_rows):
    sectors_here, block, width = wavefunction.shape
    terms = left_blocks.shape[0]
    quarter = block // QUARTERS
    z_size = sec_size // X_CHIPS
    dma = pltpu.SemaphoreType.DMA
    scratch = [
        pltpu.VMEM(left_blocks.shape, BF16),
        pltpu.VMEM(right_blocks.shape, BF16),
        pltpu.VMEM((terms * sectors_here * block, width), BF16),
    ]
    scratch += [pltpu.VMEM((ZERO_SLOT + 1, quarter, width), BF16) for _ in range(PRODUCTS * QUARTERS)]
    scratch += [pltpu.VMEM((sectors_here, quarter, width), BF16) for _ in range(QUARTERS)]
    scratch += [pltpu.VMEM((PRODUCTS, QUARTERS, quarter, width), BF16)] * 2
    scratch += [pltpu.VMEM((PRODUCTS, 3, quarter, width), BF16)] * 2
    scratch += [
        pltpu.VMEM((2, quarter, width), F32),
        pltpu.VMEM((quarter, width), F32),
        pltpu.VMEM((quarter, width), F32),
    ]
    rounds = PRODUCTS + 1
    scratch += [pltpu.VMEM((count, 8, 128), F32) for count in (op_size, X_CHIPS, z_size) for _ in range(rounds)]
    scratch += [pltpu.VMEM((quarter, width), BF16) for _ in range(PRODUCTS)]
    scratch += [
        dma((10 + PRODUCTS,)),
        dma((rounds, QUARTERS, 3, 2)),
        dma((rounds, QUARTERS, 3, 2)),
        dma((PRODUCTS, QUARTERS)),
        dma((PRODUCTS, 3)),
        dma((rounds, 64)),
        dma((rounds, op_size)),
        dma((rounds, X_CHIPS)),
        dma((rounds, z_size)),
        dma((rounds, op_size + X_CHIPS + z_size)),
    ]
    smem = pl.BlockSpec(memory_space=pltpu.SMEM)
    hbm = pl.BlockSpec(memory_space=pl.ANY)
    vmem = pl.BlockSpec(memory_space=pltpu.VMEM)
    vector, coefs = pl.pallas_call(
        functools.partial(lanczos_kernel, sec_size, op_size),
        out_shape=(
            jax.ShapeDtypeStruct(wavefunction.shape, BF16),
            jax.ShapeDtypeStruct((2, PRODUCTS), F32),
        ),
        in_specs=[smem, smem, hbm, hbm, hbm],
        out_specs=(vmem, vmem),
        scratch_shapes=scratch,
        compiler_params=pltpu.CompilerParams(
            collective_id=0, has_side_effects=True, vmem_limit_bytes=56 * 1024 * 1024
        ),
    )(charge_shifts, sector_rows, wavefunction, left_blocks, right_blocks)
    return vector, coefs


def solution(mesh):
    in_specs = (P("sec", None, None), P("op", "sec", None, None), P("op", None, None), P("op"), P())
    out_specs = (P("sec", None, None), P())
    return jax.shard_map(
        functools.partial(on_device, mesh.shape["sec"], mesh.shape["op"]),
        mesh=mesh, in_specs=in_specs, out_specs=out_specs, check_vma=False,
    )
```

```python
import functools

import jax
import jax.numpy as jnp
from jax import lax
from jax.experimental import pallas as pl
from jax.experimental.pallas import tpu as pltpu
from jax.sharding import PartitionSpec as P

MESH = pl.DeviceIdType.MESH
PRODUCTS = 3
F32 = jnp.float32
BF16 = jnp.bfloat16
QUARTERS = 4
ZERO_SLOT = 6
X_CHIPS = 4


class Places:
    def __init__(self, sec_size, op_size):
        self.sec_size, self.op_size = sec_size, op_size
        self.sec = lax.axis_index("sec")
        self.op = lax.axis_index("op")
        self.y, self.core = self.op // 2, self.op % 2
        self.z, self.x = self.sec // X_CHIPS, self.sec % X_CHIPS
        self.y_size = op_size // 2
        self.z_size = sec_size // X_CHIPS

    def sibling(self):
        return (self.sec, self.y * 2 + (1 - self.core))

    def along_y(self, step):
        return (self.sec, ((self.y + step + self.y_size) % self.y_size) * 2 + self.core)

    def along_sec(self, step):
        return ((self.sec + step + self.sec_size) % self.sec_size, self.op)

    def op_peer(self, step):
        return (self.op + step) % self.op_size

    def x_peer(self, step):
        return (self.x + step) % X_CHIPS

    def z_peer(self, step):
        return (self.z + step) % self.z_size


def lanczos_kernel(
    sec_size, op_size, shift_ref, rows_ref, wave_hbm, left_hbm, right_hbm, out_ref, coef_ref, *scratch
):
    scratch = list(scratch)
    take = lambda count: [scratch.pop(0) for _ in range(count)]
    left, right, parts = take(3)
    vectors = [take(QUARTERS) for _ in range(PRODUCTS)] + [take(QUARTERS)]
    sib_out, sib_in, y_out, y_in = take(4)
    shard_v, shard_h, shard_own = take(3)
    op_tiles, x_tiles, z_tiles = (take(PRODUCTS + 1) for _ in range(3))
    own = [None] + [take(2) for _ in range(PRODUCTS)]
    load_sem, ext_sem, sib_sem, rs_sib_sem, rs_y_sem, send_sem, op_sem, x_sem, z_sem, tile_sem = take(10)
    block, width = parts.shape[0] // 8, parts.shape[1]
    quarter = block // QUARTERS
    half = quarter // 2
    at = Places(sec_size, op_size)
    core = at.core
    sent = [0] * (PRODUCTS + 1)

    def row_start(r):
        return pl.multiple_of(((at.y + r) % QUARTERS) * quarter, quarter)

    def half_start(r, h):
        return pl.multiple_of(((at.y + r) % QUARTERS) * quarter + h * half, half)

    loads = []
    for r in range(QUARTERS):
        for n, sector in enumerate((core, 1 - core)):
            loads.append(
                pltpu.make_async_copy(
                    wave_hbm.at[sector, pl.ds(row_start(r), quarter), :],
                    vectors[0][r].at[n * 3],
                    load_sem.at[2 * r + n],
                )
            )
    loads.append(pltpu.make_async_copy(right_hbm, right, load_sem.at[8]))
    loads.append(pltpu.make_async_copy(left_hbm, left, load_sem.at[9]))
    for copy in loads:
        copy.start()

    for k in range(PRODUCTS):
        for r in range(QUARTERS):
            vectors[k][r][ZERO_SLOT] = jnp.zeros((quarter, width), BF16)
    for copy in loads[:8]:
        copy.wait()

    barrier = pltpu.get_barrier_semaphore()
    partners = [(at.sec, at.op_peer(s)) for s in range(1, op_size)]
    partners += [(at.z * X_CHIPS + at.x_peer(s), at.op) for s in range(1, X_CHIPS)]
    partners += [(at.z_peer(s) * X_CHIPS + at.x, at.op) for s in range(1, at.z_size)]
    partners += [at.along_sec(1), at.along_sec(-1)]
    for partner in partners:
        pl.semaphore_signal(barrier, inc=1, device_id=partner, device_id_type=MESH)

    live_rows = lax.fori_loop(0, rows_ref.shape[0], lambda i, total: total + rows_ref[i], jnp.int32(0))
    live = jnp.full((1, 1), live_rows * width, jnp.int32).astype(F32)
    my_rows = rows_ref[2 * at.sec + core]

    pl.semaphore_wait(barrier, len(partners))

    flying = []

    def remote(src, dst, to, recv, pool):
        return pltpu.make_async_remote_copy(
            src_ref=src, dst_ref=dst, send_sem=send_sem.at[pool, sent[pool]], recv_sem=recv, device_id=to,
            device_id_type=MESH,
        )

    def launch(copy, pool):
        copy.start()
        flying.append(copy)
        sent[pool] += 1

    def piece(k, r, j, h):
        return vectors[k][r].at[j, pl.ds(h * half, half), :]

    def slot(k, side, mine):
        return side + (0 if mine else 3 if k < PRODUCTS else 1)

    def send_piece(k, side, r, h, kind):
        src = piece(k, r, slot(k, side, True), h)
        if k > 0 and side == 0 and r == 0:
            src = own[k][h]
        if kind == "sib":
            to, r_to, side_to, sem = at.sibling(), r, side, sib_sem
        elif kind == "y+":
            to, r_to, side_to, sem = at.along_y(1), (r - 1) % QUARTERS, side, ext_sem
        elif kind == "y-":
            to, r_to, side_to, sem = at.along_y(-1), (r + 1) % QUARTERS, side, ext_sem
        elif kind == "x+":
            to, r_to, side_to, sem = at.along_sec(1), r, 1, ext_sem
        else:
            to, r_to, side_to, sem = at.along_sec(-1), r, 2, ext_sem
        dst = piece(k, r_to, slot(k, side_to, kind != "sib"), h)
        launch(remote(src, dst, to, sem.at[k, r_to, side_to, h], k), k)

    def wait_piece(k, side, r, h, sem, mine):
        here = piece(k, r, slot(k, side, mine), h)
        remote(here, here, at.sibling(), sem.at[k, r, side, h], k).wait_recv()

    def arrive(k, side, r, h, kinds):
        wait_piece(k, side, r, h, ext_sem, True)
        for kind in kinds:
            send_piece(k, side, r, h, kind)

    def right_products(k, r):
        first = row_start(r)
        ids = first + lax.broadcasted_iota(jnp.int32, (quarter, 1), 0)

        def body(term):
            for target in range(2):
                shift = shift_ref[term]
                source = 2 * at.sec + target - shift
                valid = jnp.logical_and(source >= 0, source < 2 * sec_size)
                offset = target - shift
                side = jnp.where(offset < 0, 1, jnp.where(offset > 1, 2, 0))
                j = jnp.where((offset + 2) % 2 == core, side, side + 3)
                j = jnp.where(valid, j, ZERO_SLOT)
                value = jnp.dot(vectors[k][r][j], right[term], preferred_element_type=F32)
                if k == 0:
                    limit = rows_ref[jnp.clip(source, 0, 2 * sec_size - 1)]
                    value = jnp.where(ids < limit, value, 0.0)
                place = pl.multiple_of((term * 2 + target) * block + first, quarter)
                parts[pl.ds(place, quarter), :] = value.astype(BF16)

        for term in range(4):
            body(term)

    def left_products(target, picks):
        total = None
        for term in range(4):
            rows = [left[term, target, pl.ds(half_start(r, h), half), :] for r, h in picks]
            place = pl.multiple_of((term * 2 + target) * block, block)
            value = jnp.dot(
                jnp.concatenate(rows, axis=0), parts[pl.ds(place, block), :], preferred_element_type=F32
            )
            total = value if total is None else total + value
        return total

    def fold(value):
        folded = value[0:8]
        for i in range(8, value.shape[0], 8):
            folded = folded + value[i : i + 8]
        total = folded[:, 0:128]
        for i in range(128, width, 128):
            total = total + folded[:, i : i + 128]
        return total

    tile_count = [0] * (PRODUCTS + 1)

    def spread(tiles, sem, n, tile, count, partner):
        tiles[n][0] = tile
        for s in range(1, count):
            copy = pltpu.make_async_remote_copy(
                src_ref=tiles[n].at[0], dst_ref=tiles[n].at[count - s], send_sem=tile_sem.at[n, tile_count[n]],
                recv_sem=sem.at[n, count - s], device_id=partner(s), device_id_type=MESH,
            )
            copy.start()
            flying.append(copy)
            tile_count[n] += 1

    def gathered(tiles, sem, n, count, me):
        for s in range(1, count):
            pltpu.make_async_remote_copy(
                src_ref=tiles[n].at[s], dst_ref=tiles[n].at[s], send_sem=tile_sem.at[n, 0],
                recv_sem=sem.at[n, s], device_id=at.sibling(), device_id_type=MESH,
            ).wait_recv()
        total = None
        for i in range(count):
            tile = tiles[n][(i + count - me) % count]
            total = tile if total is None else total + tile
        return total

    def reduce_op(n, sums):
        tile = jnp.concatenate([jnp.sum(s, axis=0, keepdims=True) for s in sums], axis=0)
        tile = jnp.concatenate([tile, jnp.zeros((8 - len(sums), 128), F32)], axis=0)
        spread(op_tiles, op_sem, n, tile, op_size, lambda s: (at.sec, at.op_peer(s)))

    def reduce_x(n):
        tile = gathered(op_tiles, op_sem, n, op_size, at.op)
        spread(x_tiles, x_sem, n, tile, X_CHIPS, lambda s: (at.z * X_CHIPS + at.x_peer(s), at.op))

    def reduce_z(n):
        tile = gathered(x_tiles, x_sem, n, X_CHIPS, at.x)
        spread(z_tiles, z_sem, n, tile, at.z_size, lambda s: (at.z_peer(s) * X_CHIPS + at.x, at.op))

    def reduced(n):
        sums = jnp.sum(gathered(z_tiles, z_sem, n, at.z_size, at.z), axis=1, keepdims=True)
        return [sums[q : q + 1] / live for q in range(4)]

    step_rows = min(32, half)
    zero_sum = jnp.zeros((8, 128), F32)

    def blocks(h, body, carry):
        for first in range(0, half, step_rows):
            start = h * half + first
            ids = at.y * quarter + start + lax.broadcasted_iota(jnp.int32, (step_rows, 1), 0)
            carry = body(h, first, pl.ds(start, step_rows), ids < my_rows, carry)
        return carry

    halo_y = {0: lambda r, h: r in (1, 3), 1: lambda r, h: r in (1, 3) and h == 1}
    via_y = lambda k, r, h: halo_y[min(k, 1)](r, h)

    for h in range(2):
        for kind in ("x+", "x-"):
            send_piece(0, 0, 0, h, kind)
    for h in range(2):
        for kind in ("x+", "x-"):
            send_piece(0, 0, 2, h, kind)

    def start_sum(h, first, rows, alive, carry):
        value = jnp.where(alive, vectors[0][0][0, rows, :].astype(F32), 0.0)
        return carry + fold(value * value)

    norm = blocks(1, start_sum, blocks(0, start_sum, zero_sum))
    reduce_op(0, [norm, zero_sum, zero_sum, zero_sum])

    def halo_first(k):
        for h in range(2):
            for side in (1, 2):
                kinds = ["y+", "y-"] if via_y(k, 1, h) else []
                arrive(k, side, 0, h, kinds + ["sib"])

    def halo_rest(k, rs):
        for h in range(2):
            for r in rs:
                for side in (1, 2):
                    arrive(k, side, r, h, ["sib"])

    def from_sibling(k, sides, r):
        for side in sides:
            for h in range(2):
                wait_piece(k, side, r, h, sib_sem, False)

    alphas, betas, kept = [], [], []
    shift_a = scale_b = guess = None
    combos = []
    for k in range(PRODUCTS):
        sides = (1, 2) if k == 0 else (0, 1, 2)
        if k > 0:
            for h in range(2):
                arrive(k, 0, 3, h, (["y+"] if h == 0 else []) + ([] if via_y(k, 3, h) else ["x+", "x-"]) + ["sib"])
                arrive(k, 0, 1, h, (["y-"] if h == 1 else []) + ([] if via_y(k, 1, h) else ["x+", "x-"]) + ["sib"])
        halo_first(k)
        if k > 0:
            for h in range(2):
                arrive(k, 0, 2, h, ["x+", "x-", "sib"])
        reduce_x(k)
        from_sibling(k, sides, 0)
        for copy in kept:
            copy.wait()
        if k == 0:
            loads[8].wait()
        right_products(k, 0)
        halo_rest(k, (1, 3))
        reduce_z(k)
        from_sibling(k, sides, 1)
        right_products(k, 1)
        from_sibling(k, sides, 3)
        halo_rest(k, (2,))
        right_products(k, 3)
        from_sibling(k, sides, 2)
        right_products(k, 2)
        if k == 0:
            loads[9].wait()

        groups = (((2, 0), (1, 0)), ((3, 0), (0, 0)), ((2, 1), (1, 1)), ((3, 1), (0, 1)))

        def for_sibling(g):
            sib_out[k, g] = left_products(1 - core, groups[g]).astype(BF16)
            launch(remote(sib_out.at[k, g], sib_in.at[k, g], at.sibling(), rs_sib_sem.at[k, g], k), k)

        def for_chip(g):
            value = left_products(core, groups[g])
            remote(sib_in.at[k, g], sib_in.at[k, g], at.sibling(), rs_sib_sem.at[k, g], k).wait_recv()
            value = value + sib_in[k, g].astype(F32)
            for i, (r, h) in enumerate(groups[g]):
                part = value[i * half : (i + 1) * half]
                if r == 0:
                    shard_own[h * half : (h + 1) * half, :] = part
                else:
                    y_out[k, h * 3 + r - 1] = part.astype(BF16)
                    theirs = h * 3 + 3 - r
                    launch(
                        remote(
                            y_out.at[k, h * 3 + r - 1], y_in.at[k, theirs], at.along_y(r), rs_y_sem.at[k, theirs], k
                        ),
                        k,
                    )

        for_sibling(0)
        for_sibling(1)
        for_chip(0)
        for_sibling(2)
        for_chip(1)
        for_sibling(3)
        for_chip(2)
        for_chip(3)

        s = reduced(k)
        if k == 0:
            a, b = jnp.zeros((1, 1), F32), jnp.sqrt(s[0])
            guess = jnp.zeros((1, 1), F32)
            next_guess = guess
        else:
            alpha = s[0]
            a = alpha - guess
            b = jnp.sqrt(s[1] - 2.0 * a * s[2] + a * a * s[3])
            alphas.append(alpha)
            betas.append(b)
            next_guess = alpha
        inv_b = 1.0 / b
        combos.append((a, inv_b))
        beta = betas[-1] if k > 0 else jnp.zeros((1, 1), F32)
        guess = next_guess

        def shard_step(h, first, rows, alive, carry):
            product = shard_own[rows, :]
            for i in range(3):
                product = product + y_in[k, h * 3 + i, pl.ds(first, step_rows), :].astype(F32)
            product = jnp.where(alive, product, 0.0)
            u = (vectors[0][0][0, rows, :] if k == 0 else own[k][h][pl.ds(first, step_rows), :]).astype(F32)
            if k == 0:
                v = jnp.where(alive, u, 0.0) * inv_b
                image = product * inv_b
                new = image
            else:
                v_before = shard_v[(k - 1) % 2, rows, :]
                v = (u - a * v_before) * inv_b
                image = (product - a * shard_h[rows, :]) * inv_b
                new = image - guess * v - beta * v_before
            shard_v[k % 2, rows, :] = v
            shard_h[rows, :] = image
            new = new.astype(BF16)
            own[k + 1][h][pl.ds(first, step_rows), :] = new
            new = new.astype(F32)
            pairs = ((v, image), (new, new), (new, v), (v, v))
            return tuple(c + fold(p * q) for c, (p, q) in zip(carry, pairs))

        kinds = ("y+", "y-", "x+", "x-", "sib") if k + 1 < PRODUCTS else ("y+", "y-", "sib")
        sums = (zero_sum,) * 4
        kept = []
        for h in range(2):
            for i in range(3):
                here = y_in.at[k, h * 3 + i]
                remote(here, here, at.sibling(), rs_y_sem.at[k, h * 3 + i], k).wait_recv()
            sums = blocks(h, shard_step, sums)
            for kind in kinds:
                send_piece(k + 1, 0, 0, h, kind)
            kept.append(
                pltpu.make_async_copy(
                    own[k + 1][h], vectors[k + 1][0].at[0, pl.ds(h * half, half), :], load_sem.at[10 + 2 * k + h]
                )
            )
            kept[h].start()
        reduce_op(k + 1, sums)

    n = PRODUCTS
    arrive(n, 0, 3, 0, ["y+", "sib"])
    arrive(n, 0, 1, 0, ["sib"])
    reduce_x(n)
    arrive(n, 0, 3, 1, ["sib"])
    arrive(n, 0, 1, 1, ["y-", "sib"])
    reduce_z(n)
    for h in range(2):
        arrive(n, 0, 2, h, ["sib"])
    for r in range(QUARTERS):
        from_sibling(n, (0,), r)
    for copy in kept:
        copy.wait()
    s = reduced(n)
    a = s[0] - guess
    b = jnp.sqrt(s[1] - 2.0 * a * s[2] + a * a * s[3])
    alphas.append(s[0])
    betas.append(b)
    combos.append((a, 1.0 / b))

    weights = [None] * 4
    factor = combos[3][1]
    weights[3] = factor
    for i in (2, 1, 0):
        factor = -factor * combos[i + 1][0] * combos[i][1]
        weights[i] = factor
    for r in range(QUARTERS):
        first = row_start(r)
        for n, t in enumerate((core, 1 - core)):
            limit = rows_ref[2 * at.sec + t]

            def final(i, carry, r=r, n=n, t=t, limit=limit, first=first):
                rows = pl.ds(pl.multiple_of(i * step_rows, step_rows), step_rows)
                ids = first + i * step_rows + lax.broadcasted_iota(jnp.int32, (step_rows, 1), 0)
                value = jnp.where(ids < limit, vectors[0][r][3 * n, rows, :].astype(F32), 0.0) * weights[0]
                for m in (1, 2):
                    value = value + vectors[m][r][3 * n, rows, :].astype(F32) * weights[m]
                value = value + vectors[3][r][n, rows, :].astype(F32) * weights[3]
                out_ref[t, pl.ds(pl.multiple_of(first + i * step_rows, step_rows), step_rows), :] = value.astype(BF16)
                return carry

            lax.fori_loop(0, quarter // step_rows, final, 0)

    row = lax.broadcasted_iota(jnp.int32, (8, 128), 0)
    lane = lax.broadcasted_iota(jnp.int32, (8, 128), 1)
    coefs = jnp.zeros((8, 128), F32)
    for i in range(PRODUCTS):
        coefs = jnp.where((row == 0) & (lane == i), alphas[i], coefs)
        coefs = jnp.where((row == 1) & (lane == i), betas[i], coefs)
    coef_ref[...] = coefs[0:2, 0:PRODUCTS]

    for copy in flying:
        copy.wait_send()


def hand_over(vector_in, coefs_in, vector_out, coefs_out, held, sems):
    sectors, rows = held.shape[0], held.shape[1] // 2
    places = [(s, pl.ds(i * rows, rows)) for s in range(sectors) for i in range(2)]
    reads = [pltpu.make_async_copy(vector_in.at[p], held.at[p], sems.at[0, i]) for i, p in enumerate(places)]
    writes = [pltpu.make_async_copy(held.at[p], vector_out.at[p], sems.at[1, i]) for i, p in enumerate(places)]
    for read in reads:
        read.start()
    coefs_out[...] = coefs_in[...]
    for read, write in zip(reads, writes):
        read.wait()
        write.start()
    for write in writes:
        write.wait()


def on_device(sec_size, op_size, wavefunction, left_blocks, right_blocks, charge_shifts, sector_rows):
    sectors_here, block, width = wavefunction.shape
    terms = left_blocks.shape[0]
    quarter = block // QUARTERS
    z_size = sec_size // X_CHIPS
    dma = pltpu.SemaphoreType.DMA
    scratch = [
        pltpu.VMEM(left_blocks.shape, BF16),
        pltpu.VMEM(right_blocks.shape, BF16),
        pltpu.VMEM((terms * sectors_here * block, width), BF16),
    ]
    scratch += [pltpu.VMEM((ZERO_SLOT + 1, quarter, width), BF16) for _ in range(PRODUCTS * QUARTERS)]
    scratch += [pltpu.VMEM((sectors_here, quarter, width), BF16) for _ in range(QUARTERS)]
    scratch += [pltpu.VMEM((PRODUCTS, QUARTERS, quarter, width), BF16)] * 2
    scratch += [pltpu.VMEM((PRODUCTS, 6, quarter // 2, width), BF16)] * 2
    scratch += [
        pltpu.VMEM((2, quarter, width), F32),
        pltpu.VMEM((quarter, width), F32),
        pltpu.VMEM((quarter, width), F32),
    ]
    rounds = PRODUCTS + 1
    scratch += [pltpu.VMEM((count, 8, 128), F32) for count in (op_size, X_CHIPS, z_size) for _ in range(rounds)]
    scratch += [pltpu.VMEM((quarter // 2, width), BF16) for _ in range(2 * PRODUCTS)]
    scratch += [
        dma((10 + 2 * PRODUCTS,)),
        dma((rounds, QUARTERS, 3, 2)),
        dma((rounds, QUARTERS, 3, 2)),
        dma((PRODUCTS, QUARTERS)),
        dma((PRODUCTS, 6)),
        dma((rounds, 64)),
        dma((rounds, op_size)),
        dma((rounds, X_CHIPS)),
        dma((rounds, z_size)),
        dma((rounds, op_size + X_CHIPS + z_size)),
    ]
    smem = pl.BlockSpec(memory_space=pltpu.SMEM)
    hbm = pl.BlockSpec(memory_space=pl.ANY)
    vmem = pl.BlockSpec(memory_space=pltpu.VMEM)
    vector, coefs = pl.pallas_call(
        functools.partial(lanczos_kernel, sec_size, op_size),
        out_shape=(
            jax.ShapeDtypeStruct(wavefunction.shape, BF16),
            jax.ShapeDtypeStruct((2, PRODUCTS), F32),
        ),
        in_specs=[smem, smem, hbm, hbm, hbm],
        out_specs=(vmem, vmem),
        scratch_shapes=scratch,
        compiler_params=pltpu.CompilerParams(
            collective_id=0, has_side_effects=True, vmem_limit_bytes=56 * 1024 * 1024
        ),
    )(charge_shifts, sector_rows, wavefunction, left_blocks, right_blocks)
    return pl.pallas_call(
        hand_over,
        out_shape=(
            jax.ShapeDtypeStruct(wavefunction.shape, BF16),
            jax.ShapeDtypeStruct((2, PRODUCTS), F32),
        ),
        in_specs=[hbm, vmem],
        out_specs=(hbm, vmem),
        scratch_shapes=[pltpu.VMEM(wavefunction.shape, BF16), dma((2, 4))],
    )(vector, coefs)


def solution(mesh):
    in_specs = (P("sec", None, None), P("op", "sec", None, None), P("op", None, None), P("op"), P())
    out_specs = (P("sec", None, None), P())
    return jax.shard_map(
        functools.partial(on_device, mesh.shape["sec"], mesh.shape["op"]),
        mesh=mesh, in_specs=in_specs, out_specs=out_specs, check_vma=False,
    )
```

```python
import functools

import jax
import jax.numpy as jnp
from jax import lax
from jax.experimental import pallas as pl
from jax.experimental.pallas import tpu as pltpu
from jax.sharding import PartitionSpec as P

MESH = pl.DeviceIdType.MESH
PRODUCTS = 3
F32 = jnp.float32
BF16 = jnp.bfloat16
QUARTERS = 4
ZERO_SLOT = 6
X_CHIPS = 4


class Places:
    def __init__(self, sec_size, op_size):
        self.sec_size, self.op_size = sec_size, op_size
        self.sec = lax.axis_index("sec")
        self.op = lax.axis_index("op")
        self.y, self.core = self.op // 2, self.op % 2
        self.z, self.x = self.sec // X_CHIPS, self.sec % X_CHIPS
        self.y_size = op_size // 2
        self.z_size = sec_size // X_CHIPS

    def sibling(self):
        return (self.sec, self.y * 2 + (1 - self.core))

    def along_y(self, step):
        return (self.sec, ((self.y + step + self.y_size) % self.y_size) * 2 + self.core)

    def along_sec(self, step):
        return ((self.sec + step + self.sec_size) % self.sec_size, self.op)

    def op_peer(self, step):
        return (self.op + step) % self.op_size

    def x_peer(self, step):
        return (self.x + step) % X_CHIPS

    def z_peer(self, step):
        return (self.z + step) % self.z_size


def lanczos_kernel(
    sec_size, op_size, shift_ref, rows_ref, wave_hbm, left_hbm, right_hbm, out_ref, coef_ref, *scratch
):
    scratch = list(scratch)
    take = lambda count: [scratch.pop(0) for _ in range(count)]
    left, right, parts = take(3)
    vectors = [take(QUARTERS) for _ in range(PRODUCTS)] + [take(QUARTERS)]
    sib_out, sib_in, y_out, y_in = take(4)
    shard_v, shard_h, shard_own = take(3)
    op_tiles, x_tiles, z_tiles = (take(PRODUCTS + 1) for _ in range(3))
    before = take(QUARTERS)
    own = [None] + [take(2) for _ in range(PRODUCTS)]
    load_sem, ext_sem, sib_sem, rs_sib_sem, rs_y_sem, send_sem, op_sem, x_sem, z_sem, tile_sem = take(10)
    block, width = parts.shape[0] // 8, parts.shape[1]
    quarter = block // QUARTERS
    half = quarter // 2
    at = Places(sec_size, op_size)
    core = at.core
    sent = [0] * (PRODUCTS + 1)

    def row_start(r):
        return pl.multiple_of(((at.y + r) % QUARTERS) * quarter, quarter)

    def half_start(r, h):
        return pl.multiple_of(((at.y + r) % QUARTERS) * quarter + h * half, half)

    loads = []
    for r in range(QUARTERS):
        for n, sector in enumerate((core, 1 - core)):
            loads.append(
                pltpu.make_async_copy(
                    wave_hbm.at[sector, pl.ds(row_start(r), quarter), :],
                    vectors[0][r].at[n * 3],
                    load_sem.at[2 * r + n],
                )
            )
    loads.append(pltpu.make_async_copy(right_hbm, right, load_sem.at[8]))
    loads.append(pltpu.make_async_copy(left_hbm, left, load_sem.at[9]))
    for copy in loads:
        copy.start()

    for k in range(PRODUCTS):
        for r in range(QUARTERS):
            vectors[k][r][ZERO_SLOT] = jnp.zeros((quarter, width), BF16)
    for copy in loads[:8]:
        copy.wait()

    barrier = pltpu.get_barrier_semaphore()
    partners = [(at.sec, at.op_peer(s)) for s in range(1, op_size)]
    partners += [(at.z * X_CHIPS + at.x_peer(s), at.op) for s in range(1, X_CHIPS)]
    partners += [(at.z_peer(s) * X_CHIPS + at.x, at.op) for s in range(1, at.z_size)]
    partners += [at.along_sec(1), at.along_sec(-1)]
    for partner in partners:
        pl.semaphore_signal(barrier, inc=1, device_id=partner, device_id_type=MESH)

    live_rows = lax.fori_loop(0, rows_ref.shape[0], lambda i, total: total + rows_ref[i], jnp.int32(0))
    live = jnp.full((1, 1), live_rows * width, jnp.int32).astype(F32)
    my_rows = rows_ref[2 * at.sec + core]

    pl.semaphore_wait(barrier, len(partners))

    flying = []

    def remote(src, dst, to, recv, pool):
        return pltpu.make_async_remote_copy(
            src_ref=src, dst_ref=dst, send_sem=send_sem.at[pool, sent[pool]], recv_sem=recv, device_id=to,
            device_id_type=MESH,
        )

    def launch(copy, pool):
        copy.start()
        flying.append(copy)
        sent[pool] += 1

    def piece(k, r, j, h):
        return vectors[k][r].at[j, pl.ds(h * half, half), :]

    def slot(k, side, mine):
        return side + (0 if mine else 3 if k < PRODUCTS else 1)

    def send_piece(k, side, r, h, kind):
        src = piece(k, r, slot(k, side, True), h)
        if k > 0 and side == 0 and r == 0:
            src = own[k][h]
        if kind == "sib":
            to, r_to, side_to, sem = at.sibling(), r, side, sib_sem
        elif kind == "y+":
            to, r_to, side_to, sem = at.along_y(1), (r - 1) % QUARTERS, side, ext_sem
        elif kind == "y-":
            to, r_to, side_to, sem = at.along_y(-1), (r + 1) % QUARTERS, side, ext_sem
        elif kind == "x+":
            to, r_to, side_to, sem = at.along_sec(1), r, 1, ext_sem
        else:
            to, r_to, side_to, sem = at.along_sec(-1), r, 2, ext_sem
        dst = piece(k, r_to, slot(k, side_to, kind != "sib"), h)
        launch(remote(src, dst, to, sem.at[k, r_to, side_to, h], k), k)

    def wait_piece(k, side, r, h, sem, mine):
        here = piece(k, r, slot(k, side, mine), h)
        remote(here, here, at.sibling(), sem.at[k, r, side, h], k).wait_recv()

    def arrive(k, side, r, h, kinds):
        wait_piece(k, side, r, h, ext_sem, True)
        for kind in kinds:
            send_piece(k, side, r, h, kind)

    def right_products(k, r):
        first = row_start(r)
        ids = first + lax.broadcasted_iota(jnp.int32, (quarter, 1), 0)

        def body(term):
            for target in range(2):
                shift = shift_ref[term]
                source = 2 * at.sec + target - shift
                valid = jnp.logical_and(source >= 0, source < 2 * sec_size)
                offset = target - shift
                side = jnp.where(offset < 0, 1, jnp.where(offset > 1, 2, 0))
                j = jnp.where((offset + 2) % 2 == core, side, side + 3)
                j = jnp.where(valid, j, ZERO_SLOT)
                value = jnp.dot(vectors[k][r][j], right[term], preferred_element_type=F32)
                if k == 0:
                    limit = rows_ref[jnp.clip(source, 0, 2 * sec_size - 1)]
                    value = jnp.where(ids < limit, value, 0.0)
                place = pl.multiple_of((term * 2 + target) * block + first, quarter)
                parts[pl.ds(place, quarter), :] = value.astype(BF16)

        for term in range(4):
            body(term)

    def left_products(target, picks):
        total = None
        for term in range(4):
            rows = [left[term, target, pl.ds(half_start(r, h), half), :] for r, h in picks]
            place = pl.multiple_of((term * 2 + target) * block, block)
            value = jnp.dot(
                jnp.concatenate(rows, axis=0), parts[pl.ds(place, block), :], preferred_element_type=F32
            )
            total = value if total is None else total + value
        return total

    def fold(value):
        folded = value[0:8]
        for i in range(8, value.shape[0], 8):
            folded = folded + value[i : i + 8]
        total = folded[:, 0:128]
        for i in range(128, width, 128):
            total = total + folded[:, i : i + 128]
        return total

    tile_count = [0] * (PRODUCTS + 1)

    def spread(tiles, sem, n, tile, count, partner):
        tiles[n][0] = tile
        for s in range(1, count):
            copy = pltpu.make_async_remote_copy(
                src_ref=tiles[n].at[0], dst_ref=tiles[n].at[count - s], send_sem=tile_sem.at[n, tile_count[n]],
                recv_sem=sem.at[n, count - s], device_id=partner(s), device_id_type=MESH,
            )
            copy.start()
            flying.append(copy)
            tile_count[n] += 1

    def gathered(tiles, sem, n, count, me):
        for s in range(1, count):
            pltpu.make_async_remote_copy(
                src_ref=tiles[n].at[s], dst_ref=tiles[n].at[s], send_sem=tile_sem.at[n, 0],
                recv_sem=sem.at[n, s], device_id=at.sibling(), device_id_type=MESH,
            ).wait_recv()
        total = None
        for i in range(count):
            tile = tiles[n][(i + count - me) % count]
            total = tile if total is None else total + tile
        return total

    def reduce_op(n, sums):
        tile = jnp.concatenate([jnp.sum(s, axis=0, keepdims=True) for s in sums], axis=0)
        tile = jnp.concatenate([tile, jnp.zeros((8 - len(sums), 128), F32)], axis=0)
        spread(op_tiles, op_sem, n, tile, op_size, lambda s: (at.sec, at.op_peer(s)))

    def reduce_x(n):
        tile = gathered(op_tiles, op_sem, n, op_size, at.op)
        spread(x_tiles, x_sem, n, tile, X_CHIPS, lambda s: (at.z * X_CHIPS + at.x_peer(s), at.op))

    def reduce_z(n):
        tile = gathered(x_tiles, x_sem, n, X_CHIPS, at.x)
        spread(z_tiles, z_sem, n, tile, at.z_size, lambda s: (at.z_peer(s) * X_CHIPS + at.x, at.op))

    def reduced(n):
        sums = jnp.sum(gathered(z_tiles, z_sem, n, at.z_size, at.z), axis=1, keepdims=True)
        return [sums[q : q + 1] / live for q in range(4)]

    step_rows = min(32, half)
    zero_sum = jnp.zeros((8, 128), F32)

    def blocks(h, body, carry):
        for first in range(0, half, step_rows):
            start = h * half + first
            ids = at.y * quarter + start + lax.broadcasted_iota(jnp.int32, (step_rows, 1), 0)
            carry = body(h, first, pl.ds(start, step_rows), ids < my_rows, carry)
        return carry

    via_y = lambda r, h: r in (1, 3) and h == 1

    for r, h in ((0, 1), (0, 0), (1, 0), (3, 0), (2, 0), (2, 1)):
        for kind in ("x+", "x-"):
            send_piece(0, 0, r, h, kind)

    def start_sum(h, first, rows, alive, carry):
        value = jnp.where(alive, vectors[0][0][0, rows, :].astype(F32), 0.0)
        return carry + fold(value * value)

    norm = blocks(1, start_sum, blocks(0, start_sum, zero_sum))
    reduce_op(0, [norm, zero_sum, zero_sum, zero_sum])

    def halo_first(k):
        for h in (1, 0) if k == 0 else (0, 1):
            for side in (1, 2):
                kinds = ["y+", "y-"] if via_y(1, h) else []
                arrive(k, side, 0, h, kinds + ["sib"])

    def halo_rest(k, rs):
        for h in range(2):
            for r in rs:
                for side in (1, 2):
                    arrive(k, side, r, h, ["sib"])

    def from_sibling(k, sides, r):
        for side in sides:
            for h in range(2):
                wait_piece(k, side, r, h, sib_sem, False)

    alphas, betas, kept = [], [], []
    shift_a = scale_b = guess = None
    combos = []
    for k in range(PRODUCTS):
        sides = (1, 2) if k == 0 else (0, 1, 2)
        if k > 0:
            for h in range(2):
                arrive(k, 0, 3, h, (["y+"] if h == 0 else []) + ([] if via_y(3, h) else ["x+", "x-"]) + ["sib"])
                arrive(k, 0, 1, h, (["y-"] if h == 1 else []) + ([] if via_y(1, h) else ["x+", "x-"]) + ["sib"])
        halo_first(k)
        if k > 0:
            for h in range(2):
                arrive(k, 0, 2, h, ["x+", "x-", "sib"])
        reduce_x(k)
        from_sibling(k, sides, 0)
        for copy in kept:
            copy.wait()
        if k == 0:
            loads[8].wait()
        right_products(k, 0)
        halo_rest(k, (1, 3))
        reduce_z(k)
        from_sibling(k, sides, 1)
        right_products(k, 1)
        from_sibling(k, sides, 3)
        halo_rest(k, (2,))
        right_products(k, 3)
        from_sibling(k, sides, 2)
        right_products(k, 2)
        if k == 0:
            loads[9].wait()

        groups = (((2, 0), (1, 0)), ((3, 0), (0, 0)), ((2, 1), (1, 1)), ((3, 1), (0, 1)))

        def for_sibling(g):
            sib_out[k, g] = left_products(1 - core, groups[g]).astype(BF16)
            launch(remote(sib_out.at[k, g], sib_in.at[k, g], at.sibling(), rs_sib_sem.at[k, g], k), k)

        def for_chip(g):
            value = left_products(core, groups[g])
            remote(sib_in.at[k, g], sib_in.at[k, g], at.sibling(), rs_sib_sem.at[k, g], k).wait_recv()
            value = value + sib_in[k, g].astype(F32)
            for i, (r, h) in enumerate(groups[g]):
                part = value[i * half : (i + 1) * half]
                if r == 0:
                    shard_own[h * half : (h + 1) * half, :] = part
                else:
                    y_out[k, h * 3 + r - 1] = part.astype(BF16)
                    theirs = h * 3 + 3 - r
                    launch(
                        remote(
                            y_out.at[k, h * 3 + r - 1], y_in.at[k, theirs], at.along_y(r), rs_y_sem.at[k, theirs], k
                        ),
                        k,
                    )

        for_sibling(0)
        for_sibling(1)
        for_chip(0)
        for_sibling(2)
        for_chip(1)
        for_sibling(3)
        for_chip(2)
        for_chip(3)

        s = reduced(k)
        if k == 0:
            a, b = jnp.zeros((1, 1), F32), jnp.sqrt(s[0])
            guess = jnp.zeros((1, 1), F32)
            next_guess = guess
        else:
            alpha = s[0]
            a = alpha - guess
            b = jnp.sqrt(s[1] - 2.0 * a * s[2] + a * a * s[3])
            alphas.append(alpha)
            betas.append(b)
            next_guess = alpha
        inv_b = 1.0 / b
        combos.append((a, inv_b))
        beta = betas[-1] if k > 0 else jnp.zeros((1, 1), F32)
        guess = next_guess

        def shard_step(h, first, rows, alive, carry):
            product = shard_own[rows, :]
            for i in range(3):
                product = product + y_in[k, h * 3 + i, pl.ds(first, step_rows), :].astype(F32)
            product = jnp.where(alive, product, 0.0)
            u = (vectors[0][0][0, rows, :] if k == 0 else own[k][h][pl.ds(first, step_rows), :]).astype(F32)
            if k == 0:
                v = jnp.where(alive, u, 0.0) * inv_b
                image = product * inv_b
                new = image
            else:
                v_before = shard_v[(k - 1) % 2, rows, :]
                v = (u - a * v_before) * inv_b
                image = (product - a * shard_h[rows, :]) * inv_b
                new = image - guess * v - beta * v_before
            shard_v[k % 2, rows, :] = v
            shard_h[rows, :] = image
            new = new.astype(BF16)
            own[k + 1][h][pl.ds(first, step_rows), :] = new
            new = new.astype(F32)
            pairs = ((v, image), (new, new), (new, v), (v, v))
            return tuple(c + fold(p * q) for c, (p, q) in zip(carry, pairs))

        kinds = ("y+", "y-", "x+", "x-", "sib") if k + 1 < PRODUCTS else ("y+", "y-", "sib")
        sums = (zero_sum,) * 4
        kept = []
        for h in range(2):
            for i in range(3):
                here = y_in.at[k, h * 3 + i]
                remote(here, here, at.sibling(), rs_y_sem.at[k, h * 3 + i], k).wait_recv()
            sums = blocks(h, shard_step, sums)
            if h == 1 and k + 1 == PRODUCTS:
                reduce_op(k + 1, sums)
            for kind in kinds:
                send_piece(k + 1, 0, 0, h, kind)
            kept.append(
                pltpu.make_async_copy(
                    own[k + 1][h], vectors[k + 1][0].at[0, pl.ds(h * half, half), :], load_sem.at[10 + 2 * k + h]
                )
            )
            kept[h].start()
        if k + 1 < PRODUCTS:
            reduce_op(k + 1, sums)

    weights = [None, None, combos[2][1]]
    for i in (1, 0):
        weights[i] = -weights[i + 1] * combos[i + 1][0] * combos[i][1]

    def build_before():
        for r in range(QUARTERS):
            first = row_start(r)
            for n, t in enumerate((core, 1 - core)):
                limit = rows_ref[2 * at.sec + t]

                def one(i, carry, r=r, n=n, limit=limit, first=first):
                    rows = pl.ds(pl.multiple_of(i * step_rows, step_rows), step_rows)
                    ids = first + i * step_rows + lax.broadcasted_iota(jnp.int32, (step_rows, 1), 0)
                    value = jnp.where(ids < limit, vectors[0][r][3 * n, rows, :].astype(F32), 0.0) * weights[0]
                    for m in (1, 2):
                        value = value + vectors[m][r][3 * n, rows, :].astype(F32) * weights[m]
                    before[r][n, rows, :] = value
                    return carry

                lax.fori_loop(0, quarter // step_rows, one, 0)

    n = PRODUCTS
    arrive(n, 0, 3, 0, ["y+", "sib"])
    arrive(n, 0, 1, 0, ["sib"])
    reduce_x(n)
    arrive(n, 0, 3, 1, ["sib"])
    arrive(n, 0, 1, 1, ["y-", "sib"])
    reduce_z(n)
    for h in range(2):
        arrive(n, 0, 2, h, ["sib"])
    build_before()
    for r in range(QUARTERS):
        from_sibling(n, (0,), r)
    for copy in kept:
        copy.wait()
    s = reduced(n)
    a = s[0] - guess
    b = jnp.sqrt(s[1] - 2.0 * a * s[2] + a * a * s[3])
    alphas.append(s[0])
    betas.append(b)
    combos.append((a, 1.0 / b))

    def each_block(body):
        for r in range(QUARTERS):
            first = row_start(r)
            for n, t in enumerate((core, 1 - core)):

                def one(i, carry, r=r, n=n, t=t, first=first):
                    rows = pl.ds(pl.multiple_of(i * step_rows, step_rows), step_rows)
                    body(r, n, t, rows, pl.multiple_of(first + i * step_rows, step_rows))
                    return carry

                lax.fori_loop(0, quarter // step_rows, one, 0)

    last_scale = combos[3][1]
    last_shift = combos[3][0]

    def last(r, n, t, rows, place):
        value = vectors[3][r][n, rows, :].astype(F32) - last_shift * before[r][n, rows, :]
        out_ref[t, pl.ds(place, step_rows), :] = (value * last_scale).astype(BF16)

    each_block(last)

    row = lax.broadcasted_iota(jnp.int32, (8, 128), 0)
    lane = lax.broadcasted_iota(jnp.int32, (8, 128), 1)
    coefs = jnp.zeros((8, 128), F32)
    for i in range(PRODUCTS):
        coefs = jnp.where((row == 0) & (lane == i), alphas[i], coefs)
        coefs = jnp.where((row == 1) & (lane == i), betas[i], coefs)
    coef_ref[...] = coefs[0:2, 0:PRODUCTS]

    for copy in flying:
        copy.wait_send()


def on_device(sec_size, op_size, wavefunction, left_blocks, right_blocks, charge_shifts, sector_rows):
    sectors_here, block, width = wavefunction.shape
    terms = left_blocks.shape[0]
    quarter = block // QUARTERS
    z_size = sec_size // X_CHIPS
    dma = pltpu.SemaphoreType.DMA
    scratch = [
        pltpu.VMEM(left_blocks.shape, BF16),
        pltpu.VMEM(right_blocks.shape, BF16),
        pltpu.VMEM((terms * sectors_here * block, width), BF16),
    ]
    scratch += [pltpu.VMEM((ZERO_SLOT + 1, quarter, width), BF16) for _ in range(PRODUCTS * QUARTERS)]
    scratch += [pltpu.VMEM((sectors_here, quarter, width), BF16) for _ in range(QUARTERS)]
    scratch += [pltpu.VMEM((PRODUCTS, QUARTERS, quarter, width), BF16)] * 2
    scratch += [pltpu.VMEM((PRODUCTS, 6, quarter // 2, width), BF16)] * 2
    scratch += [
        pltpu.VMEM((2, quarter, width), F32),
        pltpu.VMEM((quarter, width), F32),
        pltpu.VMEM((quarter, width), F32),
    ]
    rounds = PRODUCTS + 1
    scratch += [pltpu.VMEM((count, 8, 128), F32) for count in (op_size, X_CHIPS, z_size) for _ in range(rounds)]
    scratch += [pltpu.VMEM((sectors_here, quarter, width), F32) for _ in range(QUARTERS)]
    scratch += [pltpu.VMEM((quarter // 2, width), BF16) for _ in range(2 * PRODUCTS)]
    scratch += [
        dma((10 + 2 * PRODUCTS,)),
        dma((rounds, QUARTERS, 3, 2)),
        dma((rounds, QUARTERS, 3, 2)),
        dma((PRODUCTS, QUARTERS)),
        dma((PRODUCTS, 6)),
        dma((rounds, 64)),
        dma((rounds, op_size)),
        dma((rounds, X_CHIPS)),
        dma((rounds, z_size)),
        dma((rounds, op_size + X_CHIPS + z_size)),
    ]
    smem = pl.BlockSpec(memory_space=pltpu.SMEM)
    hbm = pl.BlockSpec(memory_space=pl.ANY)
    vmem = pl.BlockSpec(memory_space=pltpu.VMEM)
    vector, coefs = pl.pallas_call(
        functools.partial(lanczos_kernel, sec_size, op_size),
        out_shape=(
            pltpu.VMEM(wavefunction.shape, BF16),
            pltpu.VMEM((2, PRODUCTS), F32),
        ),
        in_specs=[smem, smem, hbm, hbm, hbm],
        out_specs=(vmem, vmem),
        scratch_shapes=scratch,
        compiler_params=pltpu.CompilerParams(
            collective_id=0, has_side_effects=True, vmem_limit_bytes=56 * 1024 * 1024
        ),
    )(charge_shifts, sector_rows, wavefunction, left_blocks, right_blocks)
    return vector, coefs


def solution(mesh):
    in_specs = (P("sec", None, None), P("op", "sec", None, None), P("op", None, None), P("op"), P())
    out_specs = (P("sec", None, None), P())
    return jax.shard_map(
        functools.partial(on_device, mesh.shape["sec"], mesh.shape["op"]),
        mesh=mesh, in_specs=in_specs, out_specs=out_specs, check_vma=False,
    )
```

```python
import functools

import jax
import jax.numpy as jnp
from jax import lax
from jax.experimental import pallas as pl
from jax.experimental.pallas import tpu as pltpu
from jax.sharding import PartitionSpec as P

MESH = pl.DeviceIdType.MESH
PRODUCTS = 3
F32 = jnp.float32
BF16 = jnp.bfloat16
QUARTERS = 4
ZERO_SLOT = 6
X_CHIPS = 4


class Places:
    def __init__(self, sec_size, op_size):
        self.sec_size, self.op_size = sec_size, op_size
        self.sec = lax.axis_index("sec")
        self.op = lax.axis_index("op")
        self.y, self.core = self.op // 2, self.op % 2
        self.z, self.x = self.sec // X_CHIPS, self.sec % X_CHIPS
        self.y_size = op_size // 2
        self.z_size = sec_size // X_CHIPS

    def sibling(self):
        return (self.sec, self.y * 2 + (1 - self.core))

    def along_y(self, step):
        return (self.sec, ((self.y + step + self.y_size) % self.y_size) * 2 + self.core)

    def along_sec(self, step):
        return ((self.sec + step + self.sec_size) % self.sec_size, self.op)

    def op_peer(self, step):
        return (self.op + step) % self.op_size

    def x_peer(self, step):
        return (self.x + step) % X_CHIPS

    def z_peer(self, step):
        return (self.z + step) % self.z_size


def lanczos_kernel(
    sec_size, op_size, shift_ref, rows_ref, wave_hbm, left_hbm, right_hbm, out_ref, coef_ref, *scratch
):
    scratch = list(scratch)
    take = lambda count: [scratch.pop(0) for _ in range(count)]
    left, right, parts = take(3)
    vectors = [take(QUARTERS) for _ in range(PRODUCTS)] + [take(QUARTERS)]
    sib_out, sib_in, y_out, y_in = take(4)
    shard_v, shard_h, shard_own = take(3)
    op_tiles, x_tiles, z_tiles = (take(PRODUCTS + 1) for _ in range(3))
    before = take(QUARTERS)
    own = [None] + [take(2) for _ in range(PRODUCTS)]
    load_sem, ext_sem, sib_sem, rs_sib_sem, rs_y_sem, send_sem, op_sem, x_sem, z_sem, tile_sem = take(10)
    block, width = parts.shape[0] // 8, parts.shape[1]
    quarter = block // QUARTERS
    half = quarter // 2
    at = Places(sec_size, op_size)
    core = at.core
    sent = [0] * (PRODUCTS + 1)

    def row_start(r):
        return pl.multiple_of(((at.y + r) % QUARTERS) * quarter, quarter)

    def half_start(r, h):
        return pl.multiple_of(((at.y + r) % QUARTERS) * quarter + h * half, half)

    loads = []
    for r in range(QUARTERS):
        for n, sector in enumerate((core, 1 - core)):
            loads.append(
                pltpu.make_async_copy(
                    wave_hbm.at[sector, pl.ds(row_start(r), quarter), :],
                    vectors[0][r].at[n * 3],
                    load_sem.at[2 * r + n],
                )
            )
    loads.append(pltpu.make_async_copy(right_hbm, right, load_sem.at[8]))
    loads.append(pltpu.make_async_copy(left_hbm, left, load_sem.at[9]))
    for copy in loads:
        copy.start()

    for k in range(PRODUCTS):
        for r in range(QUARTERS):
            vectors[k][r][ZERO_SLOT] = jnp.zeros((quarter, width), BF16)

    barrier = pltpu.get_barrier_semaphore()
    partners = [(at.sec, at.op_peer(s)) for s in range(1, op_size)]
    partners += [(at.z * X_CHIPS + at.x_peer(s), at.op) for s in range(1, X_CHIPS)]
    partners += [(at.z_peer(s) * X_CHIPS + at.x, at.op) for s in range(1, at.z_size)]
    partners += [at.along_sec(1), at.along_sec(-1)]
    for partner in partners:
        pl.semaphore_signal(barrier, inc=1, device_id=partner, device_id_type=MESH)

    live_rows = lax.fori_loop(0, rows_ref.shape[0], lambda i, total: total + rows_ref[i], jnp.int32(0))
    live = jnp.full((1, 1), live_rows * width, jnp.int32).astype(F32)
    my_rows = rows_ref[2 * at.sec + core]

    for copy in loads[:8]:
        copy.wait()
    pl.semaphore_wait(barrier, len(partners))

    flying = []

    def remote(src, dst, to, recv, pool):
        return pltpu.make_async_remote_copy(
            src_ref=src, dst_ref=dst, send_sem=send_sem.at[pool, sent[pool]], recv_sem=recv, device_id=to,
            device_id_type=MESH,
        )

    def launch(copy, pool):
        copy.start()
        flying.append(copy)
        sent[pool] += 1

    def piece(k, r, j, h):
        return vectors[k][r].at[j, pl.ds(h * half, half), :]

    def slot(k, side, mine):
        return side + (0 if mine else 3 if k < PRODUCTS else 1)

    def send_piece(k, side, r, h, kind):
        src = piece(k, r, slot(k, side, True), h)
        if k > 0 and side == 0 and r == 0:
            src = own[k][h]
        if kind == "sib":
            to, r_to, side_to, sem = at.sibling(), r, side, sib_sem
        elif kind == "y+":
            to, r_to, side_to, sem = at.along_y(1), (r - 1) % QUARTERS, side, ext_sem
        elif kind == "y-":
            to, r_to, side_to, sem = at.along_y(-1), (r + 1) % QUARTERS, side, ext_sem
        elif kind == "x+":
            to, r_to, side_to, sem = at.along_sec(1), r, 1, ext_sem
        else:
            to, r_to, side_to, sem = at.along_sec(-1), r, 2, ext_sem
        dst = piece(k, r_to, slot(k, side_to, kind != "sib"), h)
        launch(remote(src, dst, to, sem.at[k, r_to, side_to, h], k), k)

    def wait_piece(k, side, r, h, sem, mine):
        here = piece(k, r, slot(k, side, mine), h)
        remote(here, here, at.sibling(), sem.at[k, r, side, h], k).wait_recv()

    def arrive(k, side, r, h, kinds):
        wait_piece(k, side, r, h, ext_sem, True)
        for kind in kinds:
            send_piece(k, side, r, h, kind)

    def right_products(k, r):
        first = row_start(r)
        ids = first + lax.broadcasted_iota(jnp.int32, (quarter, 1), 0)

        def body(term):
            for target in range(2):
                shift = shift_ref[term]
                source = 2 * at.sec + target - shift
                valid = jnp.logical_and(source >= 0, source < 2 * sec_size)
                offset = target - shift
                side = jnp.where(offset < 0, 1, jnp.where(offset > 1, 2, 0))
                j = jnp.where((offset + 2) % 2 == core, side, side + 3)
                j = jnp.where(valid, j, ZERO_SLOT)
                value = jnp.dot(vectors[k][r][j], right[term], preferred_element_type=F32)
                if k == 0:
                    limit = rows_ref[jnp.clip(source, 0, 2 * sec_size - 1)]
                    value = jnp.where(ids < limit, value, 0.0)
                place = pl.multiple_of((term * 2 + target) * block + first, quarter)
                parts[pl.ds(place, quarter), :] = value.astype(BF16)

        for term in range(4):
            body(term)

    def left_products(target, picks):
        total = None
        for term in range(4):
            rows = [left[term, target, pl.ds(half_start(r, h), half), :] for r, h in picks]
            place = pl.multiple_of((term * 2 + target) * block, block)
            value = jnp.dot(
                jnp.concatenate(rows, axis=0), parts[pl.ds(place, block), :], preferred_element_type=F32
            )
            total = value if total is None else total + value
        return total

    def fold(value):
        folded = value[0:8]
        for i in range(8, value.shape[0], 8):
            folded = folded + value[i : i + 8]
        total = folded[:, 0:128]
        for i in range(128, width, 128):
            total = total + folded[:, i : i + 128]
        return total

    tile_count = [0] * (PRODUCTS + 1)

    def spread(tiles, sem, n, tile, count, partner):
        tiles[n][0] = tile
        for s in range(1, count):
            copy = pltpu.make_async_remote_copy(
                src_ref=tiles[n].at[0], dst_ref=tiles[n].at[count - s], send_sem=tile_sem.at[n, tile_count[n]],
                recv_sem=sem.at[n, count - s], device_id=partner(s), device_id_type=MESH,
            )
            copy.start()
            flying.append(copy)
            tile_count[n] += 1

    def gathered(tiles, sem, n, count, me):
        for s in range(1, count):
            pltpu.make_async_remote_copy(
                src_ref=tiles[n].at[s], dst_ref=tiles[n].at[s], send_sem=tile_sem.at[n, 0],
                recv_sem=sem.at[n, s], device_id=at.sibling(), device_id_type=MESH,
            ).wait_recv()
        total = None
        for i in range(count):
            tile = tiles[n][(i + count - me) % count]
            total = tile if total is None else total + tile
        return total

    def reduce_op(n, sums):
        tile = jnp.concatenate([jnp.sum(s, axis=0, keepdims=True) for s in sums], axis=0)
        tile = jnp.concatenate([tile, jnp.zeros((8 - len(sums), 128), F32)], axis=0)
        spread(op_tiles, op_sem, n, tile, op_size, lambda s: (at.sec, at.op_peer(s)))

    def reduce_x(n):
        tile = gathered(op_tiles, op_sem, n, op_size, at.op)
        spread(x_tiles, x_sem, n, tile, X_CHIPS, lambda s: (at.z * X_CHIPS + at.x_peer(s), at.op))

    def reduce_z(n):
        tile = gathered(x_tiles, x_sem, n, X_CHIPS, at.x)
        spread(z_tiles, z_sem, n, tile, at.z_size, lambda s: (at.z_peer(s) * X_CHIPS + at.x, at.op))

    def reduced(n):
        sums = jnp.sum(gathered(z_tiles, z_sem, n, at.z_size, at.z), axis=1, keepdims=True)
        return [sums[q : q + 1] / live for q in range(4)]

    step_rows = min(32, half)
    zero_sum = jnp.zeros((8, 128), F32)

    def blocks(h, body, carry):
        for first in range(0, half, step_rows):
            start = h * half + first
            ids = at.y * quarter + start + lax.broadcasted_iota(jnp.int32, (step_rows, 1), 0)
            carry = body(h, first, pl.ds(start, step_rows), ids < my_rows, carry)
        return carry

    via_y = lambda r, h: r in (1, 3) and h == 1

    for r, h in ((0, 1), (0, 0), (1, 0), (3, 0), (2, 0), (2, 1)):
        for kind in ("x+", "x-"):
            send_piece(0, 0, r, h, kind)

    def start_sum(h, first, rows, alive, carry):
        value = jnp.where(alive, vectors[0][0][0, rows, :].astype(F32), 0.0)
        return carry + fold(value * value)

    norm = blocks(1, start_sum, blocks(0, start_sum, zero_sum))
    reduce_op(0, [norm, zero_sum, zero_sum, zero_sum])

    def halo_first(k):
        for h in (1, 0) if k == 0 else (0, 1):
            for side in (1, 2):
                kinds = ["y+", "y-"] if via_y(1, h) else []
                arrive(k, side, 0, h, kinds + ["sib"])

    def halo_rest(k, rs):
        for h in range(2):
            for r in rs:
                for side in (1, 2):
                    arrive(k, side, r, h, ["sib"])

    def from_sibling(k, sides, r):
        for side in sides:
            for h in range(2):
                wait_piece(k, side, r, h, sib_sem, False)

    alphas, betas, kept = [], [], []
    shift_a = scale_b = guess = None
    combos = []
    for k in range(PRODUCTS):
        sides = (1, 2) if k == 0 else (0, 1, 2)
        if k > 0:
            for h in range(2):
                arrive(k, 0, 3, h, (["y+"] if h == 0 else []) + ([] if via_y(3, h) else ["x+", "x-"]) + ["sib"])
                arrive(k, 0, 1, h, (["y-"] if h == 1 else []) + ([] if via_y(1, h) else ["x+", "x-"]) + ["sib"])
        halo_first(k)
        if k > 0:
            for h in range(2):
                arrive(k, 0, 2, h, ["x+", "x-", "sib"])
        reduce_x(k)
        from_sibling(k, sides, 0)
        for copy in kept:
            copy.wait()
        if k == 0:
            loads[8].wait()
        right_products(k, 0)
        halo_rest(k, (1, 3))
        reduce_z(k)
        from_sibling(k, sides, 1)
        right_products(k, 1)
        from_sibling(k, sides, 3)
        halo_rest(k, (2,))
        right_products(k, 3)
        from_sibling(k, sides, 2)
        right_products(k, 2)
        if k == 0:
            loads[9].wait()

        groups = (((2, 0), (1, 0)), ((3, 0), (0, 0)), ((2, 1), (1, 1)), ((3, 1), (0, 1)))

        def for_sibling(g):
            sib_out[k, g] = left_products(1 - core, groups[g]).astype(BF16)
            launch(remote(sib_out.at[k, g], sib_in.at[k, g], at.sibling(), rs_sib_sem.at[k, g], k), k)

        def for_chip(g):
            value = left_products(core, groups[g])
            remote(sib_in.at[k, g], sib_in.at[k, g], at.sibling(), rs_sib_sem.at[k, g], k).wait_recv()
            value = value + sib_in[k, g].astype(F32)
            for i, (r, h) in enumerate(groups[g]):
                part = value[i * half : (i + 1) * half]
                if r == 0:
                    shard_own[h * half : (h + 1) * half, :] = part
                else:
                    y_out[k, h * 3 + r - 1] = part.astype(BF16)
                    theirs = h * 3 + 3 - r
                    launch(
                        remote(
                            y_out.at[k, h * 3 + r - 1], y_in.at[k, theirs], at.along_y(r), rs_y_sem.at[k, theirs], k
                        ),
                        k,
                    )

        for_sibling(0)
        for_sibling(1)
        for_chip(0)
        for_sibling(2)
        for_chip(1)
        for_sibling(3)
        for_chip(2)
        for_chip(3)

        s = reduced(k)
        if k == 0:
            a, b = jnp.zeros((1, 1), F32), jnp.sqrt(s[0])
            guess = jnp.zeros((1, 1), F32)
            next_guess = guess
        else:
            alpha = s[0]
            a = alpha - guess
            b = jnp.sqrt(s[1] - 2.0 * a * s[2] + a * a * s[3])
            alphas.append(alpha)
            betas.append(b)
            next_guess = alpha
        inv_b = 1.0 / b
        combos.append((a, inv_b))
        beta = betas[-1] if k > 0 else jnp.zeros((1, 1), F32)
        guess = next_guess

        def shard_step(h, first, rows, alive, carry):
            product = shard_own[rows, :]
            for i in range(3):
                product = product + y_in[k, h * 3 + i, pl.ds(first, step_rows), :].astype(F32)
            product = jnp.where(alive, product, 0.0)
            u = (vectors[0][0][0, rows, :] if k == 0 else own[k][h][pl.ds(first, step_rows), :]).astype(F32)
            if k == 0:
                v = jnp.where(alive, u, 0.0) * inv_b
                image = product * inv_b
                new = image
            else:
                v_before = shard_v[(k - 1) % 2, rows, :]
                v = (u - a * v_before) * inv_b
                image = (product - a * shard_h[rows, :]) * inv_b
                new = image - guess * v - beta * v_before
            shard_v[k % 2, rows, :] = v
            shard_h[rows, :] = image
            new = new.astype(BF16)
            own[k + 1][h][pl.ds(first, step_rows), :] = new
            new = new.astype(F32)
            pairs = ((v, image), (new, new), (new, v), (v, v))
            return tuple(c + fold(p * q) for c, (p, q) in zip(carry, pairs))

        kinds = ("y+", "y-", "x+", "x-", "sib") if k + 1 < PRODUCTS else ("y+", "y-", "sib")
        sums = (zero_sum,) * 4
        kept = []
        for h in range(2):
            for i in range(3):
                here = y_in.at[k, h * 3 + i]
                remote(here, here, at.sibling(), rs_y_sem.at[k, h * 3 + i], k).wait_recv()
            sums = blocks(h, shard_step, sums)
            if h == 1 and k + 1 == PRODUCTS:
                reduce_op(k + 1, sums)
            for kind in kinds:
                send_piece(k + 1, 0, 0, h, kind)
            kept.append(
                pltpu.make_async_copy(
                    own[k + 1][h], vectors[k + 1][0].at[0, pl.ds(h * half, half), :], load_sem.at[10 + 2 * k + h]
                )
            )
            kept[h].start()
        if k + 1 < PRODUCTS:
            reduce_op(k + 1, sums)

    weights = [None, None, combos[2][1]]
    for i in (1, 0):
        weights[i] = -weights[i + 1] * combos[i + 1][0] * combos[i][1]

    def build_before():
        for r in range(QUARTERS):
            first = row_start(r)
            for n, t in enumerate((core, 1 - core)):
                limit = rows_ref[2 * at.sec + t]

                def one(i, carry, r=r, n=n, limit=limit, first=first):
                    rows = pl.ds(pl.multiple_of(i * step_rows, step_rows), step_rows)
                    ids = first + i * step_rows + lax.broadcasted_iota(jnp.int32, (step_rows, 1), 0)
                    value = jnp.where(ids < limit, vectors[0][r][3 * n, rows, :].astype(F32), 0.0) * weights[0]
                    for m in (1, 2):
                        value = value + vectors[m][r][3 * n, rows, :].astype(F32) * weights[m]
                    before[r][n, rows, :] = value
                    return carry

                lax.fori_loop(0, quarter // step_rows, one, 0)

    n = PRODUCTS
    arrive(n, 0, 3, 0, ["y+", "sib"])
    arrive(n, 0, 1, 0, ["sib"])
    reduce_x(n)
    arrive(n, 0, 3, 1, ["sib"])
    arrive(n, 0, 1, 1, ["y-", "sib"])
    reduce_z(n)
    for h in range(2):
        arrive(n, 0, 2, h, ["sib"])
    build_before()
    for r in range(QUARTERS):
        from_sibling(n, (0,), r)
    for copy in kept:
        copy.wait()
    s = reduced(n)
    a = s[0] - guess
    b = jnp.sqrt(s[1] - 2.0 * a * s[2] + a * a * s[3])
    alphas.append(s[0])
    betas.append(b)
    combos.append((a, 1.0 / b))

    def each_block(body):
        for r in range(QUARTERS):
            first = row_start(r)
            for n, t in enumerate((core, 1 - core)):

                def one(i, carry, r=r, n=n, t=t, first=first):
                    rows = pl.ds(pl.multiple_of(i * step_rows, step_rows), step_rows)
                    body(r, n, t, rows, pl.multiple_of(first + i * step_rows, step_rows))
                    return carry

                lax.fori_loop(0, quarter // step_rows, one, 0)

    last_scale = combos[3][1]
    last_shift = combos[3][0]

    def last(r, n, t, rows, place):
        value = vectors[3][r][n, rows, :].astype(F32) - last_shift * before[r][n, rows, :]
        out_ref[t, pl.ds(place, step_rows), :] = (value * last_scale).astype(BF16)

    each_block(last)

    row = lax.broadcasted_iota(jnp.int32, (8, 128), 0)
    lane = lax.broadcasted_iota(jnp.int32, (8, 128), 1)
    coefs = jnp.zeros((8, 128), F32)
    for i in range(PRODUCTS):
        coefs = jnp.where((row == 0) & (lane == i), alphas[i], coefs)
        coefs = jnp.where((row == 1) & (lane == i), betas[i], coefs)
    coef_ref[...] = coefs[0:2, 0:PRODUCTS]

    for copy in flying:
        copy.wait_send()


def on_device(sec_size, op_size, wavefunction, left_blocks, right_blocks, charge_shifts, sector_rows):
    sectors_here, block, width = wavefunction.shape
    terms = left_blocks.shape[0]
    quarter = block // QUARTERS
    z_size = sec_size // X_CHIPS
    dma = pltpu.SemaphoreType.DMA
    scratch = [
        pltpu.VMEM(left_blocks.shape, BF16),
        pltpu.VMEM(right_blocks.shape, BF16),
        pltpu.VMEM((terms * sectors_here * block, width), BF16),
    ]
    scratch += [pltpu.VMEM((ZERO_SLOT + 1, quarter, width), BF16) for _ in range(PRODUCTS * QUARTERS)]
    scratch += [pltpu.VMEM((sectors_here, quarter, width), BF16) for _ in range(QUARTERS)]
    scratch += [pltpu.VMEM((PRODUCTS, QUARTERS, quarter, width), BF16)] * 2
    scratch += [pltpu.VMEM((PRODUCTS, 6, quarter // 2, width), BF16)] * 2
    scratch += [
        pltpu.VMEM((2, quarter, width), F32),
        pltpu.VMEM((quarter, width), F32),
        pltpu.VMEM((quarter, width), F32),
    ]
    rounds = PRODUCTS + 1
    scratch += [pltpu.VMEM((count, 8, 128), F32) for count in (op_size, X_CHIPS, z_size) for _ in range(rounds)]
    scratch += [pltpu.VMEM((sectors_here, quarter, width), F32) for _ in range(QUARTERS)]
    scratch += [pltpu.VMEM((quarter // 2, width), BF16) for _ in range(2 * PRODUCTS)]
    scratch += [
        dma((10 + 2 * PRODUCTS,)),
        dma((rounds, QUARTERS, 3, 2)),
        dma((rounds, QUARTERS, 3, 2)),
        dma((PRODUCTS, QUARTERS)),
        dma((PRODUCTS, 6)),
        dma((rounds, 64)),
        dma((rounds, op_size)),
        dma((rounds, X_CHIPS)),
        dma((rounds, z_size)),
        dma((rounds, op_size + X_CHIPS + z_size)),
    ]
    smem = pl.BlockSpec(memory_space=pltpu.SMEM)
    hbm = pl.BlockSpec(memory_space=pl.ANY)
    vmem = pl.BlockSpec(memory_space=pltpu.VMEM)
    vector, coefs = pl.pallas_call(
        functools.partial(lanczos_kernel, sec_size, op_size),
        out_shape=(
            pltpu.VMEM(wavefunction.shape, BF16),
            pltpu.VMEM((2, PRODUCTS), F32),
        ),
        in_specs=[smem, smem, hbm, hbm, hbm],
        out_specs=(vmem, vmem),
        scratch_shapes=scratch,
        compiler_params=pltpu.CompilerParams(
            collective_id=0, has_side_effects=True, vmem_limit_bytes=56 * 1024 * 1024
        ),
    )(charge_shifts, sector_rows, wavefunction, left_blocks, right_blocks)
    return vector, coefs


def solution(mesh):
    in_specs = (P("sec", None, None), P("op", "sec", None, None), P("op", None, None), P("op"), P())
    out_specs = (P("sec", None, None), P())
    return jax.shard_map(
        functools.partial(on_device, mesh.shape["sec"], mesh.shape["op"]),
        mesh=mesh, in_specs=in_specs, out_specs=out_specs, check_vma=False,
    )
```
